32 devices in a mesh: dp: 8 (over y, x, core), mp: 4 (over z).
Axes of the slice: x: 2, y: 2, z: 4, core: 2. Of those that a mesh axis runs over, the one named last changes fastest.
Arguments:
- tokens: bfloat16 [8192, 1536], P(('dp', 'mp')), may hold values from -6 to 6
- cotangent: bfloat16 [8192, 1536], P(('dp', 'mp')), may hold values from -6 to 6
- lengths: int32 [8, 8], P('dp'), may hold values from 1 to 512, 1024 in all within a row
- granularity: int32 [8], P('dp'), may hold values from 0 to 3
- ln1_gain: float32 [1536], replicated, may hold values from 0.5 to 1.5
- ln1_bias: float32 [1536], replicated, may hold values from -1.5 to 1.5
- w_qkv: bfloat16 [1536, 3, 1536], P('dp', None, 'mp'), may hold values from -0.21875 to 0.21875
- w_out: bfloat16 [1536, 1536], P(('mp', 'dp')), may hold values from -0.4375 to 0.4375
- ln2_gain: float32 [1536], replicated, may hold values from 0.5 to 1.5
- ln2_bias: float32 [1536], replicated, may hold values from -1.5 to 1.5
- w_up: bfloat16 [1536, 6144], P('dp', 'mp'), may hold values from -0.15625 to 0.15625
- w_down: bfloat16 [6144, 1536], P(('mp', 'dp')), may hold values from -0.15625 to 0.15625
Outputs:
- output: bfloat16 [8192, 1536], P(('dp', 'mp'))
- input_grad: bfloat16 [8192, 1536], P(('dp', 'mp'))
- grad_ln1_gain: float32 [1536], replicated
- grad_ln1_bias: float32 [1536], replicated
- grad_w_qkv: float32 [1536, 3, 1536], P('dp', None, 'mp')
- grad_w_out: float32 [1536, 1536], P(('mp', 'dp'))
- grad_ln2_gain: float32 [1536], replicated
- grad_ln2_bias: float32 [1536], replicated
- grad_w_up: float32 [1536, 6144], P('dp', 'mp')
- grad_w_down: float32 [6144, 1536], P(('mp', 'dp'))
The draws below stay inside these ranges and needn't reach their ends.
Inputs may be any that keep to these rules, and one draw needn't show every extreme that they name: Row i lists the lengths of the 8 sequences packed in order into batch piece i; each row sums to 1024 and its longest sequence has exactly 512 tokens. Batch piece i uses the first 768 * 2^g hidden units of the feed-forward layer, g = granularity[i].
All inputs are finite; a program needn't handle non-finite values.
Results may differ from the reference program's by a relative error of at most 0.018.
Values may be sent and summed in bfloat16 or wider, within the bound.
No kernel may reach another device: no remote copies, remote signals or barrier semaphores. Data moves between devices by JAX's collectives and lax.ppermute only.
A program may use at most 128 MiB of HBM per device.

```python
import math
import jax
import jax.numpy as jnp
import numpy as np
from jax import lax

D = 1536
HEADS = 12
HDIM = 128
FF = 6144
PREFIX0 = 768
TOK_DEV = 1024
SEQS = 8
MAXLEN = 512
PIECES = 8
TOKENS = 8192
N_DP = 8


def plant(entries, own_key, low, largest):
    place = [jax.random.randint(jax.random.fold_in(own_key, axis), (), 0, length) for axis, length in enumerate(entries.shape)]
    longest = entries.shape.index(max(entries.shape))
    neighbour = place[:longest] + [(place[longest] + 1) % entries.shape[longest]] + place[longest + 1:]
    return entries.at[tuple(place)].set(low).at[tuple(neighbour)].set(largest)


def raised(values, stream_key, source, target, blocks, factor):
    owner, partner = [(jnp.arange(values.shape[position]) // (values.shape[position] // blocks)).reshape([-1 if axis == position else 1 for axis in range(values.ndim)]) for position in (source, target)]
    chosen = jax.random.permutation(stream_key, blocks)[partner]
    strong = (owner == chosen) | (owner == (partner + blocks // 2) % blocks)
    return jnp.where(strong, factor * values, values)


def steps_of(stream_key, shape, cuts, low, largest):
    factor_of, own = 1.0, jax.random.fold_in(stream_key, 6)
    for dim, blocks in cuts:
        draws = jnp.exp(jax.random.uniform(jax.random.fold_in(own, dim), (blocks,), jnp.float32, low / len(cuts), largest / len(cuts)))
        factor_of = factor_of * jnp.repeat(draws, shape[dim] // blocks).reshape([-1 if axis == dim else 1 for axis in range(len(shape))])
    return factor_of


def length_profile(count, total, bound, lean):
    portions = [(1 << 20) // math.isqrt(rank ** lean) + 1 for rank in range(2, count + 1)]
    surplus, counts = total - bound - (count - 1), [1] * (count - 1)
    while surplus > 0:
        free = [i for i in range(count - 1) if counts[i] < bound]
        mass, budget = sum([portions[i] for i in free]), surplus
        for i in free:
            more = min(bound - counts[i], max(1, budget * portions[i] // mass), surplus)
            counts[i] = counts[i] + more
            surplus = surplus - more
    return np.array([bound] + counts)


def uneven_parts(rng, amount, total, reach, lean):
    if amount == 2:
        one = jax.random.randint(rng, (), max(1, total - reach), min(reach, total - 1) + 1)
        return jnp.stack([one, total - one])
    sizes = jnp.asarray(length_profile(amount, total, reach, lean), jnp.int32)
    couples = (amount - 1) // 2
    source_of, taker = sizes[1:1 + 2 * couples:2], sizes[2:2 + 2 * couples:2]
    slack = jnp.minimum(source_of - 1, reach - taker)
    shifted = jax.random.randint(jax.random.fold_in(rng, 1), (couples,), 0, 1 << 20) % (slack + 1)
    sizes = sizes.at[1:1 + 2 * couples:2].set(source_of - shifted).at[2:2 + 2 * couples:2].set(taker + shifted)
    return sizes[jax.random.permutation(jax.random.fold_in(rng, 2), amount)]


def scatter_about(stream_key, dims, deviation, reach, split=(), kind=jnp.bfloat16):
    drawn = jax.random.normal(stream_key, dims, jnp.float32) * deviation
    if len(split) > 0:
        drawn = steps_of(stream_key, dims, split, -0.22, 0.18) * drawn
    return jnp.clip(drawn, min=-reach, max=reach).astype(kind)


def heavy_noise(own_key, shape, deviation, most, shards, heavy, held_as=jnp.bfloat16):
    values = deviation * jax.random.normal(own_key, shape, jnp.float32)
    if shards:
        values = values * steps_of(own_key, shape, shards, -0.22, 0.18)
    return jnp.clip(raised(values, jax.random.fold_in(own_key, 3), *heavy), -most, most).astype(held_as)


def setup_inputs(seed: int = 0) -> dict:
    key_of = jax.random.split(jax.random.key(seed), 13)
    return {
        "tokens": scatter_about(key_of[0], (TOKENS, D), 1.0, 6.0, ((0, 32),)),
        "cotangent": heavy_noise(key_of[1], (TOKENS, D), 1.0, 6.0, ((0, 32),), (0, 1, 32, 2.75)),
        "lengths": jax.vmap(lambda own: uneven_parts(own, SEQS, TOK_DEV, MAXLEN, 2))(jax.random.split(key_of[2], PIECES)).reshape((PIECES, SEQS)).astype(jnp.int32),
        "granularity": plant(jax.random.randint(key_of[3], (PIECES,), 0, 4), jax.random.fold_in(key_of[3], 1), 0, 3).astype(jnp.int32),
        "ln1_gain": jnp.clip(1.0 + 0.1 * jax.random.normal(key_of[4], (D,), jnp.float32), 0.5, 1.5),
        "ln1_bias": scatter_about(key_of[5], (D,), 0.3, 1.5, (), jnp.float32),
        "w_qkv": scatter_about(key_of[6], (D, 3, HEADS * HDIM), (D // 2) ** -0.5, 0.21875, ((0, 8), (2, 4))),
        "w_out": scatter_about(key_of[7], (HEADS * HDIM, D), (HEADS * HDIM // 8) ** -0.5, 0.4375, ((0, 32),)),
        "ln2_gain": jnp.clip(1.0 + 0.1 * jax.random.normal(key_of[8], (D,), jnp.float32), 0.5, 1.5),
        "ln2_bias": scatter_about(key_of[9], (D,), 0.3, 1.5, (), jnp.float32),
        "w_up": scatter_about(key_of[10], (D, FF), D ** -0.5, 0.15625, ((0, 8), (1, 4))),
        "w_down": scatter_about(key_of[11], (FF, D), (FF // 4) ** -0.5, 0.15625, ((0, 32),)),
    }


@jax.custom_vjp
def low(v):
    return lax.optimization_barrier(v.astype(jnp.bfloat16)).astype(jnp.float32)

@jax.custom_vjp
def low_back(v):
    return v

def low_keep(v):
    return (low(v), None)

def low_pass(kept, grad):
    return (grad,)

def back_keep(v):
    return (v, None)

def back_low(kept, grad):
    return (low(grad),)
low.defvjp(low_keep, low_pass)
low_back.defvjp(back_keep, back_low)
EPSILON = 1e-05
MASKED = -1e+30

def matmul_high(left, right):
    return jnp.dot(left, right, precision=lax.Precision.HIGHEST, preferred_element_type=jnp.float32)

def layer_norm(values, norm_gain, norm_bias):
    center = values - lax.optimization_barrier(jnp.mean(values, axis=-1, keepdims=True))
    spread = lax.optimization_barrier(jnp.mean(center * center, axis=-1, keepdims=True))
    return center * lax.rsqrt(spread + EPSILON) * norm_gain + norm_bias

def piece_layout(seq_lengths, total_rows):
    seg_ends = jnp.cumsum(seq_lengths).astype(jnp.int32)
    starts = (seg_ends - seq_lengths).astype(jnp.int32)
    places = jnp.arange(total_rows, dtype=jnp.int32)
    seg_ids = lax.optimization_barrier(jnp.sum((places[:, None] >= seg_ends[None, :]).astype(jnp.int32), axis=1)).astype(jnp.int32)
    member = seg_ids[:, None] == jnp.arange(seq_lengths.shape[0], dtype=jnp.int32)[None, :]
    offsets = lax.optimization_barrier(jnp.sum(jnp.where(member, starts[None, :], 0), axis=1)).astype(jnp.int32)
    return (seg_ids, (places - offsets).astype(jnp.int32))

def rotary_tables(positions, head_dim):
    half_dim = head_dim // 2
    frequencies = jnp.exp(jnp.arange(half_dim, dtype=jnp.float32) * (-2.0 * math.log(10000.0) / head_dim))
    angles = positions.astype(jnp.float32)[:, None] * frequencies[None, :]
    return (jnp.cos(angles), jnp.sin(angles))

def rotate(values, cosine, sine):
    half_dim = values.shape[-1] // 2
    first_half = values[..., :half_dim]
    second_half = values[..., half_dim:]
    cos_rows = cosine[:, None, :]
    sin_rows = sine[:, None, :]
    return jnp.concatenate([first_half * cos_rows - second_half * sin_rows, second_half * cos_rows + first_half * sin_rows], axis=-1)

def layer_forward(token_rows, gain_one, bias_one, weight_qkv, weight_out, gain_two, bias_two, weight_up, weight_down, seg_ids, positions, active_units):
    total_rows = token_rows.shape[0]
    block_rows = min(512, total_rows)
    normed_one = low(layer_norm(token_rows, gain_one, bias_one))
    projected = low_back(matmul_high(normed_one, weight_qkv.reshape(D, 3 * HEADS * HDIM)))
    projected = projected.reshape(total_rows, 3, HEADS, HDIM)
    cosine, sine = rotary_tables(positions, HDIM)
    queries = low(rotate(projected[:, 0], cosine, sine))
    keys_rot = low(rotate(projected[:, 1], cosine, sine))
    values_all = low(projected[:, 2])
    places = jnp.arange(total_rows, dtype=jnp.int32)
    score_scale = HDIM ** (-0.5)

    def attend_block(row_start):
        query_block = lax.dynamic_slice_in_dim(queries, row_start, block_rows, 0)
        seg_block = lax.dynamic_slice_in_dim(seg_ids, row_start, block_rows, 0)
        place_block = row_start + jnp.arange(block_rows, dtype=jnp.int32)
        scores = low_back(score_scale * jnp.einsum('qhd,khd->hqk', query_block, keys_rot, precision=lax.Precision.HIGHEST))
        allowed = (seg_block[:, None] == seg_ids[None, :]) & (place_block[:, None] >= places[None, :])
        scores = jnp.where(allowed[None], scores, MASKED)
        exp_scores = jnp.exp(scores - lax.optimization_barrier(jnp.max(scores, axis=-1, keepdims=True)))
        soft_weights = exp_scores / lax.optimization_barrier(jnp.sum(exp_scores, axis=-1, keepdims=True))
        return jnp.einsum('hqk,khd->qhd', low(soft_weights), values_all, precision=lax.Precision.HIGHEST)
    block_starts = jnp.arange(total_rows // block_rows, dtype=jnp.int32) * block_rows
    mixed_heads = lax.map(jax.checkpoint(attend_block), block_starts).reshape(total_rows, HEADS * HDIM)
    mixed_heads = low(low_back(mixed_heads))
    branch_attn = low_back(matmul_high(mixed_heads, weight_out))
    resid_one = token_rows + branch_attn
    normed_two = low(layer_norm(resid_one, gain_two, bias_two))
    pre_act = low_back(matmul_high(normed_two, weight_up))
    keep_units = (jnp.arange(FF, dtype=jnp.int32) < active_units).astype(jnp.float32)
    hidden_act = low(jax.nn.gelu(pre_act, approximate=True) * keep_units)
    branch_ffn = low_back(matmul_high(hidden_act, weight_down))
    return resid_one + branch_ffn

def reference(tokens, cotangent, lengths, granularity, ln1_gain, ln1_bias, w_qkv, w_out, ln2_gain, ln2_bias, w_up, w_down):
    params = tuple((weight_item.astype(jnp.float32) for weight_item in (ln1_gain, ln1_bias, w_qkv, w_out, ln2_gain, ln2_bias, w_up, w_down)))
    token_pieces = tokens.astype(jnp.float32).reshape(N_DP, TOK_DEV, D)
    cot_pieces = cotangent.astype(jnp.float32).reshape(N_DP, TOK_DEV, D)

    def piece_step(totals, piece):
        token_rows, cot_rows, piece_lengths, piece_gran = piece
        seg_ids, positions = piece_layout(piece_lengths, TOK_DEV)
        active_units = (PREFIX0 * jnp.left_shift(jnp.int32(1), piece_gran)).astype(jnp.int32)

        def apply_layer(token_arg, *weight_args):
            return layer_forward(token_arg, *weight_args, seg_ids, positions, active_units)
        result, pull_back = jax.vjp(apply_layer, token_rows, *params)
        gradients = pull_back(cot_rows)
        totals = tuple((total_item + grad_item for total_item, grad_item in zip(totals, gradients[1:])))
        return (totals, (result.astype(jnp.bfloat16), gradients[0].astype(jnp.bfloat16)))
    initial = tuple((jnp.zeros_like(weight_item) for weight_item in params))
    totals, (results, input_grads) = lax.scan(piece_step, initial, (token_pieces, cot_pieces, lengths, granularity))
    return (results.reshape(TOKENS, D), input_grads.reshape(TOKENS, D), totals[0], totals[1], totals[2], totals[3], totals[4], totals[5], totals[6], totals[7])
```

```python
import functools
import math

import jax
import jax.numpy as jnp
from jax import lax
from jax.experimental import pallas as pl
from jax.experimental.pallas import tpu as pltpu
from jax.sharding import PartitionSpec as P

HDIM = 128
PREFIX0 = 768
WINDOW = 512
EPSILON = 1e-05
MASKED = -1e30
AXES = ("dp", "mp")
F32 = jnp.float32
BF16 = jnp.bfloat16


def norm_forward(values, norm_gain, norm_bias):
    center = values - jnp.mean(values, axis=-1, keepdims=True)
    inverse = lax.rsqrt(jnp.mean(center * center, axis=-1, keepdims=True) + EPSILON)
    normalized = center * inverse
    return (normalized * norm_gain + norm_bias, normalized, inverse)


def norm_backward(upstream, normalized, inverse, norm_gain):
    scaled = upstream * norm_gain
    return inverse * (
        scaled
        - jnp.mean(scaled, axis=-1, keepdims=True)
        - normalized * jnp.mean(scaled * normalized, axis=-1, keepdims=True)
    )


def gelu_back(pre_values, upstream):
    return jax.vjp(lambda pre_value: jax.nn.gelu(pre_value, approximate=True), pre_values)[1](
        upstream
    )[0]


def dot_nt(left, right):
    return lax.dot_general(left, right, (((1,), (1,)), ((), ())), preferred_element_type=F32)


def dot_tn(left, right):
    return lax.dot_general(left, right, (((0,), (0,)), ((), ())), preferred_element_type=F32)


def dot_nn(left, right):
    return lax.dot_general(left, right, (((1,), (0,)), ((), ())), preferred_element_type=F32)


def key_range(block, rows):
    first = max(0, block * rows - (WINDOW - 1)) // rows
    return first * rows, (block + 1) * rows


def attend_kernel(heads, slots, index_ref, proj_ref, cos_ref, sin_ref, start_ref, mixed_ref, q_ref, k_ref, v_ref, lse_ref):
    index = index_ref[0]
    total = proj_ref.shape[0]
    rows = total // slots
    width = heads * HDIM
    for slot in range(slots):
        here = slice(slot * rows, (slot + 1) * rows)
        there = pl.ds(pl.multiple_of((index ^ slot) * rows, rows), rows)
        cosine, sine = cos_ref[here, :], sin_ref[here, :]
        for head in range(heads):
            for part, out in enumerate((q_ref, k_ref)):
                lane = part * width + head * HDIM
                value = proj_ref[here, lane : lane + HDIM]
                value = value * cosine + pltpu.roll(value, HDIM // 2, 1) * sine
                out[head, there, :] = value.astype(BF16)
            lane = 2 * width + head * HDIM
            v_ref[head, there, :] = proj_ref[here, lane : lane + HDIM].astype(BF16)
    for block in range(slots):
        low, high = key_range(block, rows)
        here = slice(block * rows, (block + 1) * rows)
        slot_rows = pl.ds(pl.multiple_of((index ^ block) * rows, rows), rows)
        query_place = block * rows + lax.broadcasted_iota(jnp.int32, (rows, high - low), 0)
        key_place = low + lax.broadcasted_iota(jnp.int32, (rows, high - low), 1)
        allowed = (key_place >= start_ref[slot_rows, :]) & (key_place <= query_place)
        for head in range(heads):
            scores = dot_nt(q_ref[head, here, :], k_ref[head, low:high, :]) * (HDIM**-0.5)
            scores = jnp.where(allowed, scores, MASKED)
            top = jnp.max(scores, axis=-1, keepdims=True)
            weights = jnp.exp(scores - top)
            mass = jnp.sum(weights, axis=-1, keepdims=True)
            weights = (weights / mass).astype(BF16)
            mixed = dot_nn(weights, v_ref[head, low:high, :])
            mixed_ref[slot_rows, head * HDIM : (head + 1) * HDIM] = mixed.astype(BF16)
            lse_ref[head, here, :] = top + jnp.log(mass)


def attend_back_kernel(
    heads, slots, index_ref, grad_ref, q_ref, k_ref, v_ref, lse_ref, cos_ref, sin_ref, start_ref, out_ref, dk_ref, dv_ref
):
    index = index_ref[0]
    total = grad_ref.shape[0]
    rows = total // slots
    width = heads * HDIM
    scale = HDIM**-0.5
    dk_ref[...] = jnp.zeros_like(dk_ref)
    dv_ref[...] = jnp.zeros_like(dv_ref)
    for block in range(slots):
        low, high = key_range(block, rows)
        here = slice(block * rows, (block + 1) * rows)
        slot_rows = pl.ds(pl.multiple_of((index ^ block) * rows, rows), rows)
        query_place = block * rows + lax.broadcasted_iota(jnp.int32, (rows, high - low), 0)
        key_place = low + lax.broadcasted_iota(jnp.int32, (rows, high - low), 1)
        allowed = (key_place >= start_ref[slot_rows, :]) & (key_place <= query_place)
        cosine, sine = cos_ref[slot_rows, :], sin_ref[slot_rows, :]
        for head in range(heads):
            query = q_ref[head, here, :]
            keys = k_ref[head, low:high, :]
            values = v_ref[head, low:high, :]
            grad = grad_ref[slot_rows, head * HDIM : (head + 1) * HDIM]
            scores = jnp.where(allowed, dot_nt(query, keys) * scale, MASKED)
            probs = jnp.exp(scores - lse_ref[head, here, :])
            prob_grad = dot_nt(grad, values)
            mean = jnp.sum(probs * prob_grad, axis=-1, keepdims=True)
            score_grad = (probs * (prob_grad - mean)).astype(BF16)
            query_grad = dot_nn(score_grad, keys) * scale
            query_grad = query_grad * cosine - pltpu.roll(query_grad, HDIM // 2, 1) * sine
            out_ref[slot_rows, head * HDIM : (head + 1) * HDIM] = query_grad.astype(BF16)
            dk_ref[head, low:high, :] += dot_tn(score_grad, query)
            dv_ref[head, low:high, :] += dot_tn(probs.astype(BF16), grad)
    for slot in range(slots):
        here = slice(slot * rows, (slot + 1) * rows)
        there = pl.ds(pl.multiple_of((index ^ slot) * rows, rows), rows)
        cosine, sine = cos_ref[here, :], sin_ref[here, :]
        for head in range(heads):
            key_grad = dk_ref[head, there, :] * scale
            key_grad = key_grad * cosine - pltpu.roll(key_grad, HDIM // 2, 1) * sine
            lane = width + head * HDIM
            out_ref[here, lane : lane + HDIM] = key_grad.astype(BF16)
            lane = 2 * width + head * HDIM
            out_ref[here, lane : lane + HDIM] = dv_ref[head, there, :].astype(BF16)


def vmem():
    return pl.BlockSpec(memory_space=pltpu.VMEM)


def attend(index, proj, cosine, sine, start, heads, slots):
    total = proj.shape[0]
    shape = jax.ShapeDtypeStruct
    return pl.pallas_call(
        functools.partial(attend_kernel, heads, slots),
        in_specs=[pl.BlockSpec(memory_space=pltpu.SMEM)] + [vmem()] * 4,
        out_specs=[vmem()] * 5,
        out_shape=[
            shape((total, heads * HDIM), BF16),
            shape((heads, total, HDIM), BF16),
            shape((heads, total, HDIM), BF16),
            shape((heads, total, HDIM), BF16),
            shape((heads, total, 1), F32),
        ],
        cost_estimate=pl.CostEstimate(flops=3 * 10**9, bytes_accessed=12 * 10**6, transcendentals=2 * 10**6),
        name="attend",
    )(index, proj, cosine, sine, start)


def attend_back(index, grad, q, k, v, lse, cosine, sine, start, heads, slots):
    total = grad.shape[0]
    return pl.pallas_call(
        functools.partial(attend_back_kernel, heads, slots),
        in_specs=[pl.BlockSpec(memory_space=pltpu.SMEM)] + [vmem()] * 8,
        out_specs=vmem(),
        out_shape=jax.ShapeDtypeStruct((total, 3 * heads * HDIM), BF16),
        scratch_shapes=[pltpu.VMEM((heads, total, HDIM), F32)] * 2,
        cost_estimate=pl.CostEstimate(flops=6 * 10**9, bytes_accessed=12 * 10**6, transcendentals=2 * 10**6),
        name="attend_back",
    )(index, grad, q, k, v, lse, cosine, sine, start)


class Layout:
    def __init__(self, dp_count, mp_count):
        self.dp_count, self.mp_count = dp_count, mp_count
        self.planes = dp_count // 2
        self.groups = [[2 * plane + c for plane in range(self.planes)] for c in range(2)]

    def permute(self, value, place):
        pairs = []
        for plane in range(self.planes):
            for c in range(2):
                for p in range(2):
                    for zl in range(2):
                        target = place(plane, c, p, zl)
                        pairs.append((self.number(plane, c, p, zl), self.number(*target)))
        return lax.ppermute(value, AXES, pairs)

    def number(self, plane, c, p, zl):
        return (2 * plane + c) * self.mp_count + 2 * p + zl

    def swap(self, value):
        return self.permute(value, lambda plane, c, p, zl: (plane, p, c, zl))

    def swap_over(self, value):
        return self.permute(value, lambda plane, c, p, zl: (plane, p, 1 - c, zl))

    def swap_over_back(self, value):
        return self.permute(value, lambda plane, c, p, zl: (plane, 1 - p, c, zl))

    def core(self, value):
        return self.permute(value, lambda plane, c, p, zl: (plane, 1 - c, p, zl))

    def pair(self, value):
        return self.permute(value, lambda plane, c, p, zl: (plane, c, p, 1 - zl))

    def gather_weight(self, shard, p):
        one, two = self.swap(shard), self.swap_over(shard)
        both = jnp.where(p == 0, jnp.concatenate([one, two]), jnp.concatenate([two, one]))
        return lax.all_gather(both, "dp", axis=0, tiled=True, axis_index_groups=self.groups)

    def scatter_grad(self, grad, p):
        part = lax.psum_scatter(
            grad.astype(BF16), "dp", scatter_dimension=0, tiled=True, axis_index_groups=self.groups
        )
        half = part.shape[0] // 2
        first, second = part[:half], part[half:]
        mine = jnp.where(p == 0, first, second)
        other = jnp.where(p == 0, second, first)
        return self.swap(mine).astype(F32) + self.swap_over_back(other).astype(F32)


def on_device(
    tokens,
    cotangent,
    lengths,
    granularity,
    ln1_gain,
    ln1_bias,
    w_qkv,
    w_out,
    ln2_gain,
    ln2_bias,
    w_up,
    w_down,
):
    layout = Layout(lax.axis_size("dp"), lax.axis_size("mp"))
    slots = 4
    dp_index, mp_index = lax.axis_index("dp"), lax.axis_index("mp")
    c, p, zl = dp_index % 2, mp_index // 2, mp_index % 2
    index = 2 * c + zl
    rows = tokens.shape[0]
    total = slots * rows
    part_width = w_qkv.shape[2]
    heads = part_width // HDIM
    units = w_up.shape[1]

    facts = jnp.concatenate([lengths[0], granularity])
    facts = jnp.where(p == c, facts, layout.core(facts))
    piece_lengths, piece_gran = facts[:-1], facts[-1]

    wide_qkv = layout.gather_weight(w_qkv.reshape(w_qkv.shape[0], -1), p)
    moved_tokens = layout.swap(tokens)
    moved_cot = layout.swap(cotangent)
    wide_out = layout.gather_weight(w_out, p)
    wide_up = layout.gather_weight(w_up, p)
    wide_down = layout.gather_weight(w_down, p)

    slot_of = jnp.arange(total, dtype=jnp.int32) // rows
    places = (slot_of ^ index) * rows + jnp.arange(total, dtype=jnp.int32) % rows
    seg_ends = jnp.cumsum(piece_lengths)
    starts = seg_ends - piece_lengths
    seg_ids = jnp.sum((places[:, None] >= seg_ends[None, :]).astype(jnp.int32), axis=1)
    member = seg_ids[:, None] == jnp.arange(piece_lengths.shape[0], dtype=jnp.int32)[None, :]
    start = jnp.sum(jnp.where(member, starts[None, :], 0), axis=1)
    half = HDIM // 2
    frequencies = jnp.exp(jnp.arange(half, dtype=F32) * (-2.0 * math.log(10000.0) / HDIM))
    angles = (places - start).astype(F32)[:, None] * frequencies[None, :]
    cosine, sine = jnp.cos(angles), jnp.sin(angles)
    cosine = jnp.concatenate([cosine, cosine], axis=1)
    sine = jnp.concatenate([-sine, sine], axis=1)
    start = start[:, None]
    where = index[None]

    near_tokens = jnp.concatenate([moved_tokens, layout.pair(moved_tokens)]).astype(F32)
    near_one, unit_one, inverse_one = norm_forward(near_tokens, ln1_gain, ln1_bias)
    near_one = near_one.astype(BF16)
    inputs_one = jnp.concatenate([near_one, layout.core(near_one)])
    near_cot = jnp.concatenate([moved_cot, layout.pair(moved_cot)])
    cot_all = jnp.concatenate([near_cot, layout.core(near_cot)])

    projected = dot_nn(inputs_one, wide_qkv)
    mixed, q_all, k_all, v_all, lse = attend(where, projected, cosine, sine, start, heads, slots)

    def chip_sum(part):
        part = part.astype(F32)
        return part[: 2 * rows] + layout.core(part[2 * rows :].astype(BF16)).astype(F32)

    def pair_sum(chip):
        other = layout.pair(chip.astype(BF16)).astype(F32)
        return chip + jnp.concatenate([other[rows:], other[:rows]])

    def pair_own(chip):
        return chip[:rows] + layout.pair(chip[rows:].astype(BF16)).astype(F32)

    resid_one = near_tokens + pair_sum(chip_sum(dot_nn(mixed, wide_out)))
    near_two, unit_two, inverse_two = norm_forward(resid_one, ln2_gain, ln2_bias)
    near_two = near_two.astype(BF16)
    inputs_two = jnp.concatenate([near_two, layout.core(near_two)])

    prefix = PREFIX0 * jnp.left_shift(jnp.int32(1), piece_gran)
    active_units = jnp.clip(prefix - index * units, 0, units)
    keep_units = (jnp.arange(units, dtype=jnp.int32) < active_units).astype(F32)
    pre_act = dot_nn(inputs_two, wide_up)
    hidden_act = (jax.nn.gelu(pre_act, approximate=True) * keep_units).astype(BF16)
    hidden_grad = dot_nt(cot_all, wide_down)
    pre_grad = (gelu_back(pre_act, hidden_grad) * keep_units).astype(BF16)
    near_two_grad = pair_sum(chip_sum(dot_nt(pre_grad, wide_up)))

    output = resid_one[:rows] + pair_own(chip_sum(dot_nn(hidden_act, wide_down)))
    output = layout.swap(output.astype(BF16))
    grad_down = layout.scatter_grad(dot_tn(hidden_act, cot_all), p)
    grad_up = layout.scatter_grad(dot_tn(inputs_two, pre_grad), p)

    resid_grad = near_cot.astype(F32) + norm_backward(near_two_grad, unit_two, inverse_two, ln2_gain)
    gain_two_grad = jnp.sum(near_two_grad[:rows] * unit_two[:rows], axis=0)
    bias_two_grad = jnp.sum(near_two_grad[:rows], axis=0)
    resid_low = resid_grad.astype(BF16)
    resid_all = jnp.concatenate([resid_low, layout.core(resid_low)])
    mixed_grad = dot_nt(resid_all, wide_out).astype(BF16)
    grad_out = layout.scatter_grad(dot_tn(mixed, resid_all), p)
    projected_grad = attend_back(where, mixed_grad, q_all, k_all, v_all, lse, cosine, sine, start, heads, slots)
    own_one_grad = pair_own(chip_sum(dot_nt(projected_grad, wide_qkv)))
    grad_qkv = layout.scatter_grad(dot_tn(inputs_one, projected_grad), p)
    input_grad = resid_grad[:rows] + norm_backward(own_one_grad, unit_one[:rows], inverse_one[:rows], ln1_gain)
    input_grad = layout.swap(input_grad.astype(BF16))
    gain_one_grad = jnp.sum(own_one_grad * unit_one[:rows], axis=0)
    bias_one_grad = jnp.sum(own_one_grad, axis=0)
    norm_sums = lax.psum(jnp.stack([gain_one_grad, bias_one_grad, gain_two_grad, bias_two_grad]), AXES)
    return (
        output,
        input_grad,
        norm_sums[0],
        norm_sums[1],
        grad_qkv.reshape(w_qkv.shape),
        grad_out,
        norm_sums[2],
        norm_sums[3],
        grad_up,
        grad_down,
    )


def solution(mesh):
    return jax.shard_map(
        on_device,
        mesh=mesh,
        in_specs=(
            P(("dp", "mp"), None),
            P(("dp", "mp"), None),
            P("dp", None),
            P("dp"),
            P(),
            P(),
            P("dp", None, "mp"),
            P(("mp", "dp"), None),
            P(),
            P(),
            P("dp", "mp"),
            P(("mp", "dp"), None),
        ),
        out_specs=(
            P(("dp", "mp"), None),
            P(("dp", "mp"), None),
            P(),
            P(),
            P("dp", None, "mp"),
            P(("mp", "dp"), None),
            P(),
            P(),
            P("dp", "mp"),
            P(("mp", "dp"), None),
        ),
        check_vma=False,
    )
```

```python
import functools
import math

import jax
import jax.numpy as jnp
from jax import lax
from jax.experimental import pallas as pl
from jax.experimental.pallas import tpu as pltpu
from jax.sharding import PartitionSpec as P

HDIM = 128
PREFIX0 = 768
WINDOW = 512
EPSILON = 1e-05
MASKED = -1e30
AXES = ("dp", "mp")
F32 = jnp.float32
BF16 = jnp.bfloat16


def norm_forward(values, norm_gain, norm_bias):
    center = values - jnp.mean(values, axis=-1, keepdims=True)
    inverse = lax.rsqrt(jnp.mean(center * center, axis=-1, keepdims=True) + EPSILON)
    normalized = center * inverse
    return (normalized * norm_gain + norm_bias, normalized, inverse)


def norm_backward(upstream, normalized, inverse, norm_gain):
    scaled = upstream * norm_gain
    return inverse * (
        scaled
        - jnp.mean(scaled, axis=-1, keepdims=True)
        - normalized * jnp.mean(scaled * normalized, axis=-1, keepdims=True)
    )


def gelu_back(pre_values, upstream):
    return jax.vjp(lambda pre_value: jax.nn.gelu(pre_value, approximate=True), pre_values)[1](
        upstream
    )[0]


def dot_nt(left, right):
    return lax.dot_general(left, right, (((1,), (1,)), ((), ())), preferred_element_type=F32)


def dot_tn(left, right):
    return lax.dot_general(left, right, (((0,), (0,)), ((), ())), preferred_element_type=F32)


def dot_nn(left, right):
    return lax.dot_general(left, right, (((1,), (0,)), ((), ())), preferred_element_type=F32)


def key_range(block, rows):
    first = max(0, block * rows - (WINDOW - 1)) // rows
    return first * rows, (block + 1) * rows


def attend_kernel(heads, slots, index_ref, proj_ref, cos_ref, sin_ref, start_ref, mixed_ref, q_ref, k_ref, v_ref, lse_ref):
    index = index_ref[0]
    total = proj_ref.shape[0]
    rows = total // slots
    width = heads * HDIM
    for slot in range(slots):
        here = slice(slot * rows, (slot + 1) * rows)
        there = pl.ds(pl.multiple_of((index ^ slot) * rows, rows), rows)
        cosine, sine = cos_ref[here, :], sin_ref[here, :]
        for head in range(heads):
            for part, out in enumerate((q_ref, k_ref)):
                lane = part * width + head * HDIM
                value = proj_ref[here, lane : lane + HDIM]
                value = value * cosine + pltpu.roll(value, HDIM // 2, 1) * sine
                out[head, there, :] = value.astype(BF16)
            lane = 2 * width + head * HDIM
            v_ref[head, there, :] = proj_ref[here, lane : lane + HDIM].astype(BF16)
    for block in range(slots):
        low, high = key_range(block, rows)
        here = slice(block * rows, (block + 1) * rows)
        slot_rows = pl.ds(pl.multiple_of((index ^ block) * rows, rows), rows)
        query_place = block * rows + lax.broadcasted_iota(jnp.int32, (rows, high - low), 0)
        key_place = low + lax.broadcasted_iota(jnp.int32, (rows, high - low), 1)
        allowed = (key_place >= start_ref[slot_rows, :]) & (key_place <= query_place)
        for head in range(heads):
            scores = dot_nt(q_ref[head, here, :], k_ref[head, low:high, :]) * (HDIM**-0.5)
            scores = jnp.where(allowed, scores, MASKED)
            top = jnp.max(scores, axis=-1, keepdims=True)
            weights = jnp.exp(scores - top)
            mass = jnp.sum(weights, axis=-1, keepdims=True)
            weights = (weights / mass).astype(BF16)
            mixed = dot_nn(weights, v_ref[head, low:high, :])
            mixed_ref[slot_rows, head * HDIM : (head + 1) * HDIM] = mixed.astype(BF16)
            lse_ref[head, here, :] = top + jnp.log(mass)


def attend_back_kernel(
    heads, slots, index_ref, grad_ref, q_ref, k_ref, v_ref, lse_ref, cos_ref, sin_ref, start_ref, out_ref, dk_ref, dv_ref
):
    index = index_ref[0]
    total = grad_ref.shape[0]
    rows = total // slots
    width = heads * HDIM
    scale = HDIM**-0.5
    dk_ref[...] = jnp.zeros_like(dk_ref)
    dv_ref[...] = jnp.zeros_like(dv_ref)
    for block in range(slots):
        low, high = key_range(block, rows)
        here = slice(block * rows, (block + 1) * rows)
        slot_rows = pl.ds(pl.multiple_of((index ^ block) * rows, rows), rows)
        query_place = block * rows + lax.broadcasted_iota(jnp.int32, (rows, high - low), 0)
        key_place = low + lax.broadcasted_iota(jnp.int32, (rows, high - low), 1)
        allowed = (key_place >= start_ref[slot_rows, :]) & (key_place <= query_place)
        cosine, sine = cos_ref[slot_rows, :], sin_ref[slot_rows, :]
        for head in range(heads):
            query = q_ref[head, here, :]
            keys = k_ref[head, low:high, :]
            values = v_ref[head, low:high, :]
            grad = grad_ref[slot_rows, head * HDIM : (head + 1) * HDIM]
            scores = jnp.where(allowed, dot_nt(query, keys) * scale, MASKED)
            probs = jnp.exp(scores - lse_ref[head, here, :])
            prob_grad = dot_nt(grad, values)
            mean = jnp.sum(probs * prob_grad, axis=-1, keepdims=True)
            score_grad = (probs * (prob_grad - mean)).astype(BF16)
            query_grad = dot_nn(score_grad, keys) * scale
            query_grad = query_grad * cosine - pltpu.roll(query_grad, HDIM // 2, 1) * sine
            out_ref[slot_rows, head * HDIM : (head + 1) * HDIM] = query_grad.astype(BF16)
            dk_ref[head, low:high, :] += dot_tn(score_grad, query)
            dv_ref[head, low:high, :] += dot_tn(probs.astype(BF16), grad)
    for slot in range(slots):
        here = slice(slot * rows, (slot + 1) * rows)
        there = pl.ds(pl.multiple_of((index ^ slot) * rows, rows), rows)
        cosine, sine = cos_ref[here, :], sin_ref[here, :]
        for head in range(heads):
            key_grad = dk_ref[head, there, :] * scale
            key_grad = key_grad * cosine - pltpu.roll(key_grad, HDIM // 2, 1) * sine
            lane = width + head * HDIM
            out_ref[here, lane : lane + HDIM] = key_grad.astype(BF16)
            lane = 2 * width + head * HDIM
            out_ref[here, lane : lane + HDIM] = dv_ref[head, there, :].astype(BF16)


def vmem():
    return pl.BlockSpec(memory_space=pltpu.VMEM)


def attend(index, proj, cosine, sine, start, heads, slots):
    total = proj.shape[0]
    shape = jax.ShapeDtypeStruct
    return pl.pallas_call(
        functools.partial(attend_kernel, heads, slots),
        in_specs=[pl.BlockSpec(memory_space=pltpu.SMEM)] + [vmem()] * 4,
        out_specs=[vmem()] * 5,
        out_shape=[
            shape((total, heads * HDIM), BF16),
            shape((heads, total, HDIM), BF16),
            shape((heads, total, HDIM), BF16),
            shape((heads, total, HDIM), BF16),
            shape((heads, total, 1), F32),
        ],
        cost_estimate=pl.CostEstimate(flops=3 * 10**9, bytes_accessed=12 * 10**6, transcendentals=2 * 10**6),
        name="attend",
    )(index, proj, cosine, sine, start)


def attend_back(index, grad, q, k, v, lse, cosine, sine, start, heads, slots):
    total = grad.shape[0]
    return pl.pallas_call(
        functools.partial(attend_back_kernel, heads, slots),
        in_specs=[pl.BlockSpec(memory_space=pltpu.SMEM)] + [vmem()] * 8,
        out_specs=vmem(),
        out_shape=jax.ShapeDtypeStruct((total, 3 * heads * HDIM), BF16),
        scratch_shapes=[pltpu.VMEM((heads, total, HDIM), F32)] * 2,
        cost_estimate=pl.CostEstimate(flops=6 * 10**9, bytes_accessed=12 * 10**6, transcendentals=2 * 10**6),
        name="attend_back",
    )(index, grad, q, k, v, lse, cosine, sine, start)


class Layout:
    def __init__(self, dp_count, mp_count):
        self.dp_count, self.mp_count = dp_count, mp_count
        self.planes = dp_count // 2
        self.groups = [[2 * plane + c for plane in range(self.planes)] for c in range(2)]

    def permute(self, value, place):
        pairs = []
        for plane in range(self.planes):
            for c in range(2):
                for p in range(2):
                    for zl in range(2):
                        target = place(plane, c, p, zl)
                        pairs.append((self.number(plane, c, p, zl), self.number(*target)))
        return lax.ppermute(value, AXES, pairs)

    def number(self, plane, c, p, zl):
        return (2 * plane + c) * self.mp_count + 2 * p + zl

    def swap(self, value):
        return self.permute(value, lambda plane, c, p, zl: (plane, p, c, zl))

    def swap_over(self, value):
        return self.permute(value, lambda plane, c, p, zl: (plane, p, 1 - c, zl))

    def send_shard(self, shard):
        return self.swap(shard), self.swap_over(shard)

    def line_up(self, shards, p):
        one, two = shards
        return jnp.where(p == 0, jnp.concatenate([one, two]), jnp.concatenate([two, one]))

    def sum_all(self, value):
        value = value + self.core(value)
        value = value + self.pair(value)
        value = value + self.permute(value, lambda plane, c, p, zl: (plane, c, 1 - p, zl))
        step = 1
        while step < self.planes:
            value = value + self.plane_step(value, step)
            step *= 2
        return value

    def flip(self, value, into):
        pairs = []
        for plane in range(self.planes):
            for c in range(2):
                for zl in range(2):
                    near, far = self.number(plane, c, c, zl), self.number(plane, c, 1 - c, zl)
                    pairs.append((far, near) if into else (near, far))
        return lax.ppermute(value, AXES, pairs)

    def core(self, value):
        return self.permute(value, lambda plane, c, p, zl: (plane, 1 - c, p, zl))

    def pair(self, value):
        return self.permute(value, lambda plane, c, p, zl: (plane, c, p, 1 - zl))

    def plane_step(self, value, flip):
        return self.permute(value, lambda plane, c, p, zl: (plane ^ flip, c, p, zl))

    def both(self, shard, other, c):
        return jnp.where(c == 0, jnp.concatenate([shard, other]), jnp.concatenate([other, shard]))

    def gather(self, block):
        return lax.all_gather(block, "dp", axis=0, tiled=True, axis_index_groups=self.groups)

    def gather_near(self, block):
        if self.planes != 4:
            return (self.gather(block),)
        return block, self.plane_step(block, 1), self.plane_step(block, 2)

    def far_sends(self, pieces):
        if self.planes != 4:
            return ()
        half = pieces[0].shape[0] // 2
        return pieces[1][:half], pieces[2][half:]

    def gather_far(self, pieces, sends):
        if self.planes != 4:
            return pieces
        return *pieces, self.plane_step(sends[0], 2), self.plane_step(sends[1], 1)

    def assemble(self, pieces, plane):
        if self.planes != 4:
            return pieces[0]
        block, across, along, far_one, far_two = pieces
        rows = block.shape[0]
        whole = jnp.zeros((4 * rows, block.shape[1]), block.dtype)
        put = lambda whole, piece, place: lax.dynamic_update_slice(whole, piece, (place, 0))
        whole = put(whole, block, plane * rows)
        whole = put(whole, across, (plane ^ 1) * rows)
        whole = put(whole, along, (plane ^ 2) * rows)
        whole = put(whole, far_one, (plane ^ 3) * rows)
        return put(whole, far_two, (plane ^ 3) * rows + rows // 2)

    def scatter(self, grad):
        return lax.psum_scatter(grad, "dp", scatter_dimension=0, tiled=True, axis_index_groups=self.groups)

    def near_sends(self, grad, plane):
        if self.planes != 4:
            return ()
        rows = grad.shape[0] // 4
        half = rows // 2
        take = lambda place: lax.dynamic_slice(grad, (place, 0), (half, grad.shape[1]))
        return take((plane ^ 3) * rows), take((plane ^ 3) * rows + half)

    def scatter_near(self, grad, sends):
        if self.planes != 4:
            return self.scatter(grad)
        return self.plane_step(sends[0], 1), self.plane_step(sends[1], 2)

    def later_sends(self, grad, got, plane):
        if self.planes != 4:
            return ()
        rows = grad.shape[0] // 4
        half = rows // 2
        take = lambda place, count: lax.dynamic_slice(grad, (place, 0), (count, grad.shape[1]))
        add = lambda left, right: (left.astype(F32) + right.astype(F32)).astype(BF16)
        to_across = jnp.concatenate(
            [take((plane ^ 1) * rows, half), add(take((plane ^ 1) * rows + half, half), got[1])]
        )
        to_along = jnp.concatenate(
            [add(take((plane ^ 2) * rows, half), got[0]), take((plane ^ 2) * rows + half, half)]
        )
        return to_across, to_along

    def scatter_far(self, grad, got, sends, plane):
        if self.planes != 4:
            return got
        rows = grad.shape[0] // 4
        mine = lax.dynamic_slice(grad, (plane * rows, 0), (rows, grad.shape[1]))
        return mine, self.plane_step(sends[0], 1), self.plane_step(sends[1], 2)

    def scatter_sum(self, parts):
        if self.planes != 4:
            return parts
        return sum([part.astype(F32) for part in parts]).astype(BF16)

    def own_shards(self, part, received, c):
        whole = part.astype(F32) + received.astype(F32)
        first, second = jnp.split(whole, 2)
        return jnp.where(c == 0, first, second), jnp.where(c == 0, second, first)


def hold(*values):
    return lax.optimization_barrier(values)


def after(value, *others):
    return lax.optimization_barrier((value, others))[0]


def on_device(
    tokens,
    cotangent,
    lengths,
    granularity,
    ln1_gain,
    ln1_bias,
    w_qkv,
    w_out,
    ln2_gain,
    ln2_bias,
    w_up,
    w_down,
):
    layout = Layout(lax.axis_size("dp"), lax.axis_size("mp"))
    slots = 4
    dp_index, mp_index = lax.axis_index("dp"), lax.axis_index("mp")
    c, p, zl = dp_index % 2, mp_index // 2, mp_index % 2
    plane = dp_index // 2
    index = 2 * c + zl
    rows = tokens.shape[0]
    total = slots * rows
    part_width = w_qkv.shape[2]
    heads = part_width // HDIM
    units = w_up.shape[1]

    facts = jnp.concatenate([lengths[0], granularity])
    other_facts = layout.core(facts)
    facts = jnp.where(p == c, facts, other_facts)
    piece_lengths, piece_gran = facts[:-1], facts[-1]

    depth = w_qkv.shape[0]
    w_qkv_flat, _ = hold(w_qkv.reshape(depth, -1), other_facts)
    sent_qkv = layout.send_shard(w_qkv_flat)
    block_qkv = layout.line_up(sent_qkv, p)
    wide_qkv = layout.gather(block_qkv)
    moved_tokens = layout.swap(after(tokens, block_qkv))
    sent_out = layout.send_shard(after(w_out, block_qkv))
    other_down = layout.core(after(w_down, block_qkv))
    both_down = layout.both(w_down, other_down, c)

    slot_of = jnp.arange(total, dtype=jnp.int32) // rows
    places = (slot_of ^ index) * rows + jnp.arange(total, dtype=jnp.int32) % rows
    seg_ends = jnp.cumsum(piece_lengths)
    starts = seg_ends - piece_lengths
    seg_ids = jnp.sum((places[:, None] >= seg_ends[None, :]).astype(jnp.int32), axis=1)
    member = seg_ids[:, None] == jnp.arange(piece_lengths.shape[0], dtype=jnp.int32)[None, :]
    start = jnp.sum(jnp.where(member, starts[None, :], 0), axis=1)
    half = HDIM // 2
    frequencies = jnp.exp(jnp.arange(half, dtype=F32) * (-2.0 * math.log(10000.0) / HDIM))
    angles = (places - start).astype(F32)[:, None] * frequencies[None, :]
    cosine, sine = jnp.cos(angles), jnp.sin(angles)
    cosine = jnp.concatenate([cosine, cosine], axis=1)
    sine = jnp.concatenate([-sine, sine], axis=1)
    start = start[:, None]
    where = index[None]

    moved_tokens, cosine, sine, start, both_down = hold(moved_tokens, cosine, sine, start, both_down)
    pair_tokens = layout.pair(moved_tokens)
    block_out = layout.line_up(after(sent_out, moved_tokens), p)
    wide_out = layout.gather(block_out)
    pair_tokens, block_out = hold(pair_tokens, block_out)
    near_tokens = jnp.concatenate([moved_tokens, pair_tokens]).astype(F32)
    near_one, unit_one, inverse_one = norm_forward(near_tokens, ln1_gain, ln1_bias)
    near_one, w_up = hold(near_one.astype(BF16), w_up)
    sent_up = layout.send_shard(w_up)
    inputs_one = jnp.concatenate([near_one, layout.core(near_one)])
    projected = dot_nn(inputs_one, wide_qkv)
    projected, sent_up, both_down = hold(projected, sent_up, both_down)
    block_up, projected, both_down = hold(layout.line_up(sent_up, p), projected, both_down)
    pieces_up = layout.gather_near(block_up)
    flip_down = layout.flip(both_down, False)
    mixed, q_all, k_all, v_all, lse = attend(where, projected, cosine, sine, start, heads, slots)
    attn_part = dot_nn(mixed, wide_out)
    attn_send = attn_part[2 * rows :].astype(BF16)
    attn_send, pieces_up, flip_down = hold(attn_send, pieces_up, flip_down)

    attn_got = layout.core(attn_send)
    block_down = jnp.where(p == c, both_down, flip_down)
    sends_up = layout.far_sends(pieces_up)
    attn_got, block_down, sends_up = hold(attn_got, block_down, sends_up)
    wide_down = layout.gather(block_down)
    attn_chip = attn_part[: 2 * rows] + attn_got.astype(F32)
    attn_low, sends_up, cotangent = hold(attn_chip.astype(BF16), sends_up, cotangent)
    attn_other = layout.pair(attn_low)
    pieces_up = layout.gather_far(pieces_up, sends_up)
    moved_cot = layout.swap(cotangent)
    attn_other, pieces_up, moved_cot = hold(attn_other, pieces_up, moved_cot)

    def pair_order(other):
        other = other.astype(F32)
        return jnp.concatenate([other[rows:], other[:rows]])

    resid_one = near_tokens + attn_chip + pair_order(attn_other)
    near_two, unit_two, inverse_two = norm_forward(resid_one, ln2_gain, ln2_bias)
    near_two, pieces_up, moved_cot = hold(near_two.astype(BF16), pieces_up, moved_cot)
    pair_cot = layout.pair(moved_cot)
    inputs_two = jnp.concatenate([near_two, layout.core(near_two)])
    wide_up = layout.assemble(pieces_up, plane)

    prefix = PREFIX0 * jnp.left_shift(jnp.int32(1), piece_gran)
    active_units = jnp.clip(prefix - index * units, 0, units)
    keep_units = (jnp.arange(units, dtype=jnp.int32) < active_units).astype(F32)
    pre_act = dot_nn(inputs_two, wide_up)
    hidden_act = (jax.nn.gelu(pre_act, approximate=True) * keep_units).astype(BF16)
    hidden_act, pair_cot = hold(hidden_act, pair_cot)
    near_cot = jnp.concatenate([moved_cot, pair_cot])
    cot_all = jnp.concatenate([near_cot, layout.core(near_cot)])
    grad_down_part = dot_tn(hidden_act, cot_all).astype(BF16)
    grad_down_sum = layout.scatter(grad_down_part)
    wide_down = after(wide_down, grad_down_part)
    hidden_grad = dot_nt(cot_all, wide_down)
    pre_grad = (gelu_back(pre_act, hidden_grad) * keep_units).astype(BF16)
    ffn_part = dot_nt(pre_grad, wide_up)
    (ffn_send,) = hold(ffn_part[2 * rows :].astype(BF16))
    (ffn_got,) = hold(layout.core(ffn_send))
    ffn_chip = ffn_part[: 2 * rows] + ffn_got.astype(F32)
    ffn_low, pre_grad, hidden_act = hold(ffn_chip.astype(BF16), pre_grad, hidden_act)
    ffn_other = layout.pair(ffn_low)
    grad_up_part = dot_tn(inputs_two, pre_grad).astype(BF16)
    grad_up_sum = layout.scatter(grad_up_part)
    out_part = dot_nn(hidden_act, wide_down)
    out_send = out_part[2 * rows :].astype(BF16)
    ffn_other, out_send, grad_up_part = hold(ffn_other, out_send, grad_up_part)
    near_two_grad = ffn_chip + pair_order(ffn_other)

    resid_grad = near_cot.astype(F32) + norm_backward(near_two_grad, unit_two, inverse_two, ln2_gain)
    gain_two_grad = jnp.sum(near_two_grad[:rows] * unit_two[:rows], axis=0)
    bias_two_grad = jnp.sum(near_two_grad[:rows], axis=0)
    resid_low = resid_grad.astype(BF16)
    resid_low, out_send, down_sum = hold(resid_low, out_send, grad_down_sum)
    down_flip = layout.flip(down_sum, True)
    out_got = layout.core(out_send)
    resid_all = jnp.concatenate([resid_low, layout.core(resid_low)])
    mixed_grad = dot_nt(resid_all, wide_out).astype(BF16)
    grad_out_part = dot_tn(mixed, resid_all).astype(BF16)
    grad_out_sum = layout.scatter(grad_out_part)
    projected_grad = attend_back(
        where, after(mixed_grad, grad_out_part), q_all, k_all, v_all, lse, cosine, sine, start, heads, slots
    )
    grad_qkv_part = dot_tn(inputs_one, projected_grad).astype(BF16)
    near_qkv = layout.near_sends(grad_qkv_part, plane)
    out_chip = out_part[: 2 * rows] + after(out_got, near_qkv).astype(F32)
    near_qkv, down_flip, out_send, projected_grad = hold(near_qkv, down_flip, out_chip[rows:].astype(BF16), projected_grad)

    got_qkv = layout.scatter_near(grad_qkv_part, near_qkv)
    out_other = layout.pair(out_send)
    one_part = dot_nt(projected_grad, wide_qkv)
    one_send = one_part[2 * rows :].astype(BF16)
    one_send, got_qkv, out_other = hold(one_send, got_qkv, out_other)
    one_got = layout.core(one_send)
    later_qkv = layout.later_sends(grad_qkv_part, got_qkv, plane)
    one_got, later_qkv = hold(one_got, later_qkv)
    one_chip = one_part[: 2 * rows] + one_got.astype(F32)
    output = resid_one[:rows] + out_chip[:rows] + out_other.astype(F32)
    one_send, later_qkv, up_sum, output = hold(one_chip[rows:].astype(BF16), later_qkv, grad_up_sum, output.astype(BF16))
    one_other = layout.pair(one_send)
    qkv_parts = layout.scatter_far(grad_qkv_part, got_qkv, later_qkv, plane)
    up_flip = layout.flip(up_sum, True)
    down_own, down_other = layout.own_shards(down_sum, down_flip, c)
    one_other, qkv_parts, up_flip, output, down_other = hold(one_other, qkv_parts, up_flip, output, down_other)

    own_one_grad = one_chip[:rows] + one_other.astype(F32)
    gain_one_grad = jnp.sum(own_one_grad * unit_one[:rows], axis=0)
    bias_one_grad = jnp.sum(own_one_grad, axis=0)
    norm_parts = jnp.stack([gain_one_grad, bias_one_grad, gain_two_grad, bias_two_grad])
    input_grad = resid_grad[:rows] + norm_backward(own_one_grad, unit_one[:rows], inverse_one[:rows], ln1_gain)
    qkv_sum = layout.scatter_sum(qkv_parts)
    one_sum = jnp.concatenate([qkv_sum, grad_out_sum.reshape(qkv_sum.shape[0], -1)], axis=1)
    input_grad, norm_parts, one_sum, output = hold(input_grad.astype(BF16), norm_parts, one_sum, output)
    one_flip = layout.flip(one_sum, True)
    moved_input = layout.swap(input_grad)
    moved_output = layout.swap(output)
    norm_sums = layout.sum_all(norm_parts)
    up_own, up_other = layout.own_shards(up_sum, up_flip, c)
    one_flip, norm_sums, up_own, up_other = hold(one_flip, norm_sums, up_own, up_other)
    one_own, one_other = layout.own_shards(one_sum, one_flip, c)
    down_got, up_got, one_got = layout.core(down_other), layout.core(up_other), layout.core(one_other)
    grad_down = jnp.where(p == c, down_own, down_got)
    grad_up = jnp.where(p == c, up_own, up_got)
    grad_one = jnp.where(p == c, one_own, one_got)
    grad_qkv = grad_one[:, : 3 * part_width]
    grad_out = grad_one[:, 3 * part_width :].reshape(w_out.shape)
    output, input_grad = moved_output, moved_input
    return (
        output,
        input_grad,
        norm_sums[0],
        norm_sums[1],
        grad_qkv.reshape(w_qkv.shape),
        grad_out,
        norm_sums[2],
        norm_sums[3],
        grad_up,
        grad_down,
    )


def solution(mesh):
    return jax.shard_map(
        on_device,
        mesh=mesh,
        in_specs=(
            P(("dp", "mp"), None),
            P(("dp", "mp"), None),
            P("dp", None),
            P("dp"),
            P(),
            P(),
            P("dp", None, "mp"),
            P(("mp", "dp"), None),
            P(),
            P(),
            P("dp", "mp"),
            P(("mp", "dp"), None),
        ),
        out_specs=(
            P(("dp", "mp"), None),
            P(("dp", "mp"), None),
            P(),
            P(),
            P("dp", None, "mp"),
            P(("mp", "dp"), None),
            P(),
            P(),
            P("dp", "mp"),
            P(("mp", "dp"), None),
        ),
        check_vma=False,
    )
```

```python
import functools
import math

import jax
import jax.numpy as jnp
from jax import lax
from jax.experimental import pallas as pl
from jax.experimental.pallas import tpu as pltpu
from jax.sharding import PartitionSpec as P

HDIM = 128
PREFIX0 = 768
WINDOW = 512
EPSILON = 1e-05
MASKED = -1e30
AXES = ("dp", "mp")
F32 = jnp.float32
BF16 = jnp.bfloat16


def norm_forward(values, norm_gain, norm_bias):
    center = values - jnp.mean(values, axis=-1, keepdims=True)
    inverse = lax.rsqrt(jnp.mean(center * center, axis=-1, keepdims=True) + EPSILON)
    normalized = center * inverse
    return (normalized * norm_gain + norm_bias, normalized, inverse)


def norm_backward(upstream, normalized, inverse, norm_gain):
    scaled = upstream * norm_gain
    return inverse * (
        scaled
        - jnp.mean(scaled, axis=-1, keepdims=True)
        - normalized * jnp.mean(scaled * normalized, axis=-1, keepdims=True)
    )


def gelu_back(pre_values, upstream):
    return jax.vjp(lambda pre_value: jax.nn.gelu(pre_value, approximate=True), pre_values)[1](
        upstream
    )[0]


def dot_nt(left, right):
    return lax.dot_general(left, right, (((1,), (1,)), ((), ())), preferred_element_type=F32)


def dot_tn(left, right):
    return lax.dot_general(left, right, (((0,), (0,)), ((), ())), preferred_element_type=F32)


def dot_nn(left, right):
    return lax.dot_general(left, right, (((1,), (0,)), ((), ())), preferred_element_type=F32)


def key_range(block, rows):
    first = max(0, block * rows - (WINDOW - 1)) // rows
    return first * rows, (block + 1) * rows


def attend_kernel(heads, slots, index_ref, proj_ref, cos_ref, sin_ref, start_ref, mixed_ref, q_ref, k_ref, v_ref, lse_ref):
    index = index_ref[0]
    total = proj_ref.shape[0]
    rows = total // slots
    width = heads * HDIM
    for slot in range(slots):
        here = slice(slot * rows, (slot + 1) * rows)
        there = pl.ds(pl.multiple_of((index ^ slot) * rows, rows), rows)
        cosine, sine = cos_ref[here, :], sin_ref[here, :]
        for head in range(heads):
            for part, out in enumerate((q_ref, k_ref)):
                lane = part * width + head * HDIM
                value = proj_ref[here, lane : lane + HDIM]
                value = value * cosine + pltpu.roll(value, HDIM // 2, 1) * sine
                out[head, there, :] = value.astype(BF16)
            lane = 2 * width + head * HDIM
            v_ref[head, there, :] = proj_ref[here, lane : lane + HDIM].astype(BF16)
    for block in range(slots):
        low, high = key_range(block, rows)
        here = slice(block * rows, (block + 1) * rows)
        slot_rows = pl.ds(pl.multiple_of((index ^ block) * rows, rows), rows)
        query_place = block * rows + lax.broadcasted_iota(jnp.int32, (rows, high - low), 0)
        key_place = low + lax.broadcasted_iota(jnp.int32, (rows, high - low), 1)
        allowed = (key_place >= start_ref[slot_rows, :]) & (key_place <= query_place)
        for head in range(heads):
            scores = dot_nt(q_ref[head, here, :], k_ref[head, low:high, :]) * (HDIM**-0.5)
            scores = jnp.where(allowed, scores, MASKED)
            top = jnp.max(scores, axis=-1, keepdims=True)
            weights = jnp.exp(scores - top)
            mass = jnp.sum(weights, axis=-1, keepdims=True)
            weights = (weights / mass).astype(BF16)
            mixed = dot_nn(weights, v_ref[head, low:high, :])
            mixed_ref[slot_rows, head * HDIM : (head + 1) * HDIM] = mixed.astype(BF16)
            lse_ref[head, here, :] = top + jnp.log(mass)


def attend_back_kernel(
    heads, slots, index_ref, grad_ref, q_ref, k_ref, v_ref, lse_ref, cos_ref, sin_ref, start_ref, out_ref, dk_ref, dv_ref
):
    index = index_ref[0]
    total = grad_ref.shape[0]
    rows = total // slots
    width = heads * HDIM
    scale = HDIM**-0.5
    dk_ref[...] = jnp.zeros_like(dk_ref)
    dv_ref[...] = jnp.zeros_like(dv_ref)
    for block in range(slots):
        low, high = key_range(block, rows)
        here = slice(block * rows, (block + 1) * rows)
        slot_rows = pl.ds(pl.multiple_of((index ^ block) * rows, rows), rows)
        query_place = block * rows + lax.broadcasted_iota(jnp.int32, (rows, high - low), 0)
        key_place = low + lax.broadcasted_iota(jnp.int32, (rows, high - low), 1)
        allowed = (key_place >= start_ref[slot_rows, :]) & (key_place <= query_place)
        cosine, sine = cos_ref[slot_rows, :], sin_ref[slot_rows, :]
        for head in range(heads):
            query = q_ref[head, here, :]
            keys = k_ref[head, low:high, :]
            values = v_ref[head, low:high, :]
            grad = grad_ref[slot_rows, head * HDIM : (head + 1) * HDIM]
            scores = jnp.where(allowed, dot_nt(query, keys) * scale, MASKED)
            probs = jnp.exp(scores - lse_ref[head, here, :])
            prob_grad = dot_nt(grad, values)
            mean = jnp.sum(probs * prob_grad, axis=-1, keepdims=True)
            score_grad = (probs * (prob_grad - mean)).astype(BF16)
            query_grad = dot_nn(score_grad, keys) * scale
            query_grad = query_grad * cosine - pltpu.roll(query_grad, HDIM // 2, 1) * sine
            out_ref[slot_rows, head * HDIM : (head + 1) * HDIM] = query_grad.astype(BF16)
            dk_ref[head, low:high, :] += dot_tn(score_grad, query)
            dv_ref[head, low:high, :] += dot_tn(probs.astype(BF16), grad)
    for slot in range(slots):
        here = slice(slot * rows, (slot + 1) * rows)
        there = pl.ds(pl.multiple_of((index ^ slot) * rows, rows), rows)
        cosine, sine = cos_ref[here, :], sin_ref[here, :]
        for head in range(heads):
            key_grad = dk_ref[head, there, :] * scale
            key_grad = key_grad * cosine - pltpu.roll(key_grad, HDIM // 2, 1) * sine
            lane = width + head * HDIM
            out_ref[here, lane : lane + HDIM] = key_grad.astype(BF16)
            lane = 2 * width + head * HDIM
            out_ref[here, lane : lane + HDIM] = dv_ref[head, there, :].astype(BF16)


def vmem():
    return pl.BlockSpec(memory_space=pltpu.VMEM)


def attend(index, proj, cosine, sine, start, heads, slots):
    total = proj.shape[0]
    shape = jax.ShapeDtypeStruct
    return pl.pallas_call(
        functools.partial(attend_kernel, heads, slots),
        in_specs=[pl.BlockSpec(memory_space=pltpu.SMEM)] + [vmem()] * 4,
        out_specs=[vmem()] * 5,
        out_shape=[
            shape((total, heads * HDIM), BF16),
            shape((heads, total, HDIM), BF16),
            shape((heads, total, HDIM), BF16),
            shape((heads, total, HDIM), BF16),
            shape((heads, total, 1), F32),
        ],
        cost_estimate=pl.CostEstimate(flops=3 * 10**9, bytes_accessed=12 * 10**6, transcendentals=2 * 10**6),
        name="attend",
    )(index, proj, cosine, sine, start)


def attend_back(index, grad, q, k, v, lse, cosine, sine, start, heads, slots):
    total = grad.shape[0]
    return pl.pallas_call(
        functools.partial(attend_back_kernel, heads, slots),
        in_specs=[pl.BlockSpec(memory_space=pltpu.SMEM)] + [vmem()] * 8,
        out_specs=vmem(),
        out_shape=jax.ShapeDtypeStruct((total, 3 * heads * HDIM), BF16),
        scratch_shapes=[pltpu.VMEM((heads, total, HDIM), F32)] * 2,
        cost_estimate=pl.CostEstimate(flops=6 * 10**9, bytes_accessed=12 * 10**6, transcendentals=2 * 10**6),
        name="attend_back",
    )(index, grad, q, k, v, lse, cosine, sine, start)


class Layout:
    def __init__(self, dp_count, mp_count):
        self.dp_count, self.mp_count = dp_count, mp_count
        self.planes = dp_count // 2
        self.groups = [[2 * plane + c for plane in range(self.planes)] for c in range(2)]

    def permute(self, value, place):
        pairs = []
        for plane in range(self.planes):
            for c in range(2):
                for p in range(2):
                    for zl in range(2):
                        target = place(plane, c, p, zl)
                        pairs.append((self.number(plane, c, p, zl), self.number(*target)))
        return lax.ppermute(value, AXES, pairs)

    def number(self, plane, c, p, zl):
        return (2 * plane + c) * self.mp_count + 2 * p + zl

    def swap(self, value):
        return self.permute(value, lambda plane, c, p, zl: (plane, p, c, zl))

    def swap_over(self, value):
        return self.permute(value, lambda plane, c, p, zl: (plane, p, 1 - c, zl))

    def send_shard(self, shard):
        return self.swap(shard), self.swap_over(shard)

    def line_up(self, shards, p):
        one, two = shards
        return jnp.where(p == 0, jnp.concatenate([one, two]), jnp.concatenate([two, one]))

    def sum_quad(self, value):
        value = value + self.core(value)
        return value + self.pair(value)

    def sum_quads(self, value):
        value = value + self.permute(value, lambda plane, c, p, zl: (plane, c, 1 - p, zl))
        step = 1
        while step < self.planes:
            value = value + self.plane_step(value, step)
            step *= 2
        return value

    def swap_over_back(self, value):
        return self.permute(value, lambda plane, c, p, zl: (plane, 1 - p, c, zl))

    def flip(self, value, into):
        pairs = []
        for plane in range(self.planes):
            for c in range(2):
                for zl in range(2):
                    near, far = self.number(plane, c, c, zl), self.number(plane, c, 1 - c, zl)
                    pairs.append((far, near) if into else (near, far))
        return lax.ppermute(value, AXES, pairs)

    def core(self, value):
        return self.permute(value, lambda plane, c, p, zl: (plane, 1 - c, p, zl))

    def pair(self, value):
        return self.permute(value, lambda plane, c, p, zl: (plane, c, p, 1 - zl))

    def plane_step(self, value, flip):
        return self.permute(value, lambda plane, c, p, zl: (plane ^ flip, c, p, zl))

    def both(self, shard, other, c):
        return jnp.where(c == 0, jnp.concatenate([shard, other]), jnp.concatenate([other, shard]))

    def gather(self, block):
        return lax.all_gather(block, "dp", axis=0, tiled=True, axis_index_groups=self.groups)

    def gather_near(self, block):
        if self.planes != 4:
            return (self.gather(block),)
        return block, self.plane_step(block, 1), self.plane_step(block, 2)

    def far_sends(self, pieces):
        if self.planes != 4:
            return ()
        half = pieces[0].shape[0] // 2
        return pieces[1][:half], pieces[2][half:]

    def gather_far(self, pieces, sends):
        if self.planes != 4:
            return pieces
        return *pieces, self.plane_step(sends[0], 2), self.plane_step(sends[1], 1)

    def assemble(self, pieces, plane):
        if self.planes != 4:
            return pieces[0]
        block, across, along, far_one, far_two = pieces
        rows = block.shape[0]
        whole = jnp.zeros((4 * rows, block.shape[1]), block.dtype)
        put = lambda whole, piece, place: lax.dynamic_update_slice(whole, piece, (place, 0))
        whole = put(whole, block, plane * rows)
        whole = put(whole, across, (plane ^ 1) * rows)
        whole = put(whole, along, (plane ^ 2) * rows)
        whole = put(whole, far_one, (plane ^ 3) * rows)
        return put(whole, far_two, (plane ^ 3) * rows + rows // 2)

    def scatter(self, grad):
        return lax.psum_scatter(grad, "dp", scatter_dimension=0, tiled=True, axis_index_groups=self.groups)

    def near_sends(self, grad, plane):
        if self.planes != 4:
            return ()
        rows = grad.shape[0] // 4
        half = rows // 2
        take = lambda place: lax.dynamic_slice(grad, (place, 0), (half, grad.shape[1]))
        return take((plane ^ 3) * rows), take((plane ^ 3) * rows + half)

    def scatter_near(self, grad, sends):
        if self.planes != 4:
            return self.scatter(grad)
        return self.plane_step(sends[0], 1), self.plane_step(sends[1], 2)

    def later_sends(self, grad, got, plane):
        if self.planes != 4:
            return ()
        rows = grad.shape[0] // 4
        half = rows // 2
        take = lambda place, count: lax.dynamic_slice(grad, (place, 0), (count, grad.shape[1]))
        add = lambda left, right: (left.astype(F32) + right.astype(F32)).astype(BF16)
        to_across = jnp.concatenate(
            [take((plane ^ 1) * rows, half), add(take((plane ^ 1) * rows + half, half), got[1])]
        )
        to_along = jnp.concatenate(
            [add(take((plane ^ 2) * rows, half), got[0]), take((plane ^ 2) * rows + half, half)]
        )
        return to_across, to_along

    def scatter_far(self, grad, got, sends, plane):
        if self.planes != 4:
            return got
        rows = grad.shape[0] // 4
        mine = lax.dynamic_slice(grad, (plane * rows, 0), (rows, grad.shape[1]))
        return mine, self.plane_step(sends[0], 1), self.plane_step(sends[1], 2)

    def scatter_sum(self, parts):
        if self.planes != 4:
            return parts
        return sum([part.astype(F32) for part in parts]).astype(BF16)

    def own_shards(self, part, received, c):
        whole = part.astype(F32) + received.astype(F32)
        first, second = jnp.split(whole, 2)
        return jnp.where(c == 0, first, second), jnp.where(c == 0, second, first)


def hold(*values):
    return lax.optimization_barrier(values)


def after(value, *others):
    return lax.optimization_barrier((value, others))[0]


def on_device(
    tokens,
    cotangent,
    lengths,
    granularity,
    ln1_gain,
    ln1_bias,
    w_qkv,
    w_out,
    ln2_gain,
    ln2_bias,
    w_up,
    w_down,
):
    layout = Layout(lax.axis_size("dp"), lax.axis_size("mp"))
    slots = 4
    dp_index, mp_index = lax.axis_index("dp"), lax.axis_index("mp")
    c, p, zl = dp_index % 2, mp_index // 2, mp_index % 2
    plane = dp_index // 2
    index = 2 * c + zl
    rows = tokens.shape[0]
    total = slots * rows
    part_width = w_qkv.shape[2]
    heads = part_width // HDIM
    units = w_up.shape[1]

    facts = jnp.concatenate([lengths[0], granularity])
    other_facts = layout.core(facts)
    facts = jnp.where(p == c, facts, other_facts)
    piece_lengths, piece_gran = facts[:-1], facts[-1]

    depth = w_qkv.shape[0]
    w_qkv_flat, _ = hold(w_qkv.reshape(depth, -1), other_facts)
    sent_qkv = layout.send_shard(w_qkv_flat)
    block_qkv = layout.line_up(sent_qkv, p)
    wide_qkv = layout.gather(block_qkv)
    moved_tokens = layout.swap(after(tokens, block_qkv))
    sent_out = layout.send_shard(after(w_out, block_qkv))
    other_down = layout.core(after(w_down, block_qkv))
    both_down = layout.both(w_down, other_down, c)

    slot_of = jnp.arange(total, dtype=jnp.int32) // rows
    places = (slot_of ^ index) * rows + jnp.arange(total, dtype=jnp.int32) % rows
    seg_ends = jnp.cumsum(piece_lengths)
    starts = seg_ends - piece_lengths
    seg_ids = jnp.sum((places[:, None] >= seg_ends[None, :]).astype(jnp.int32), axis=1)
    member = seg_ids[:, None] == jnp.arange(piece_lengths.shape[0], dtype=jnp.int32)[None, :]
    start = jnp.sum(jnp.where(member, starts[None, :], 0), axis=1)
    half = HDIM // 2
    frequencies = jnp.exp(jnp.arange(half, dtype=F32) * (-2.0 * math.log(10000.0) / HDIM))
    angles = (places - start).astype(F32)[:, None] * frequencies[None, :]
    cosine, sine = jnp.cos(angles), jnp.sin(angles)
    cosine = jnp.concatenate([cosine, cosine], axis=1)
    sine = jnp.concatenate([-sine, sine], axis=1)
    start = start[:, None]
    where = index[None]

    moved_tokens, cosine, sine, start, both_down = hold(moved_tokens, cosine, sine, start, both_down)
    pair_tokens = layout.pair(moved_tokens)
    block_out = layout.line_up(after(sent_out, moved_tokens), p)
    wide_out = layout.gather(block_out)
    pair_tokens, block_out = hold(pair_tokens, block_out)
    near_tokens = jnp.concatenate([moved_tokens, pair_tokens]).astype(F32)
    near_one, unit_one, inverse_one = norm_forward(near_tokens, ln1_gain, ln1_bias)
    near_one, w_up = hold(near_one.astype(BF16), w_up)
    sent_up = layout.send_shard(w_up)
    inputs_one = jnp.concatenate([near_one, layout.core(near_one)])
    projected = dot_nn(inputs_one, wide_qkv)
    projected, sent_up, both_down = hold(projected, sent_up, both_down)
    block_up, projected, both_down = hold(layout.line_up(sent_up, p), projected, both_down)
    pieces_up = layout.gather_near(block_up)
    flip_down = layout.flip(both_down, False)
    mixed, q_all, k_all, v_all, lse = attend(where, projected, cosine, sine, start, heads, slots)
    attn_part = dot_nn(mixed, wide_out)
    attn_send = attn_part[2 * rows :].astype(BF16)
    attn_send, pieces_up, flip_down = hold(attn_send, pieces_up, flip_down)

    attn_got = layout.core(attn_send)
    block_down = jnp.where(p == c, both_down, flip_down)
    sends_up = layout.far_sends(pieces_up)
    attn_got, block_down, sends_up = hold(attn_got, block_down, sends_up)
    wide_down = layout.gather(block_down)
    attn_chip = attn_part[: 2 * rows] + attn_got.astype(F32)
    attn_low, sends_up, cotangent = hold(attn_chip.astype(BF16), sends_up, cotangent)
    attn_other = layout.pair(attn_low)
    pieces_up = layout.gather_far(pieces_up, sends_up)
    moved_cot = layout.swap(cotangent)
    attn_other, pieces_up, moved_cot = hold(attn_other, pieces_up, moved_cot)

    def pair_order(other):
        other = other.astype(F32)
        return jnp.concatenate([other[rows:], other[:rows]])

    resid_one = near_tokens + attn_chip + pair_order(attn_other)
    near_two, unit_two, inverse_two = norm_forward(resid_one, ln2_gain, ln2_bias)
    near_two, pieces_up, moved_cot = hold(near_two.astype(BF16), pieces_up, moved_cot)
    pair_cot = layout.pair(moved_cot)
    inputs_two = jnp.concatenate([near_two, layout.core(near_two)])
    wide_up = layout.assemble(pieces_up, plane)

    prefix = PREFIX0 * jnp.left_shift(jnp.int32(1), piece_gran)
    active_units = jnp.clip(prefix - index * units, 0, units)
    keep_units = (jnp.arange(units, dtype=jnp.int32) < active_units).astype(F32)
    pre_act = dot_nn(inputs_two, wide_up)
    hidden_act = (jax.nn.gelu(pre_act, approximate=True) * keep_units).astype(BF16)
    hidden_act, pair_cot = hold(hidden_act, pair_cot)
    near_cot = jnp.concatenate([moved_cot, pair_cot])
    cot_all = jnp.concatenate([near_cot, layout.core(near_cot)])
    grad_down_part = dot_tn(hidden_act, cot_all).astype(BF16)
    grad_down_sum = layout.scatter(grad_down_part)
    wide_down = after(wide_down, grad_down_part)
    hidden_grad = dot_nt(cot_all, wide_down)
    pre_grad = (gelu_back(pre_act, hidden_grad) * keep_units).astype(BF16)
    ffn_part = dot_nt(pre_grad, wide_up)
    (ffn_send,) = hold(ffn_part[2 * rows :].astype(BF16))
    (ffn_got,) = hold(layout.core(ffn_send))
    ffn_chip = ffn_part[: 2 * rows] + ffn_got.astype(F32)
    ffn_low, pre_grad, hidden_act = hold(ffn_chip.astype(BF16), pre_grad, hidden_act)
    ffn_other = layout.pair(ffn_low)
    grad_up_part = dot_tn(inputs_two, pre_grad).astype(BF16)
    grad_up_sum = layout.scatter(grad_up_part)
    out_part = dot_nn(hidden_act, wide_down)
    out_send = out_part[2 * rows :].astype(BF16)
    ffn_other, out_send, grad_up_part = hold(ffn_other, out_send, grad_up_part)
    near_two_grad = ffn_chip + pair_order(ffn_other)

    resid_grad = near_cot.astype(F32) + norm_backward(near_two_grad, unit_two, inverse_two, ln2_gain)
    resid_low = resid_grad.astype(BF16)
    resid_low, out_send, down_sum = hold(resid_low, out_send, grad_down_sum)
    down_flip = layout.flip(down_sum, True)
    out_got = layout.core(out_send)
    resid_all = jnp.concatenate([resid_low, layout.core(resid_low)])
    mixed_grad = dot_nt(resid_all, wide_out).astype(BF16)
    grad_out_part = dot_tn(mixed, resid_all).astype(BF16)
    grad_out_sum = layout.scatter(grad_out_part)
    out_got = after(out_got, grad_out_part)
    out_send = (out_part[rows : 2 * rows] + out_got[rows:].astype(F32)).astype(BF16)
    out_other = layout.pair(out_send)
    projected_grad = attend_back(
        where, after(mixed_grad, out_send), q_all, k_all, v_all, lse, cosine, sine, start, heads, slots
    )
    grad_qkv_part = dot_tn(inputs_one, projected_grad).astype(BF16)
    near_qkv = layout.near_sends(grad_qkv_part, plane)
    near_qkv, down_flip, out_other, projected_grad = hold(near_qkv, down_flip, out_other, projected_grad)

    got_qkv = layout.scatter_near(grad_qkv_part, near_qkv)
    one_part = dot_nt(projected_grad, wide_qkv)
    output = resid_one[:rows] + out_part[:rows] + out_got[:rows].astype(F32) + out_other.astype(F32)
    one_send, got_qkv, output = hold(one_part[2 * rows :].astype(BF16), got_qkv, output.astype(BF16))
    (one_got,) = hold(layout.core(one_send))
    one_send = (one_part[rows : 2 * rows] + one_got[rows:].astype(F32)).astype(BF16)
    one_send, got_qkv, output, near_two_grad, up_sum = hold(one_send, got_qkv, output, near_two_grad, grad_up_sum)
    one_other = layout.pair(one_send)
    later_qkv = layout.later_sends(grad_qkv_part, got_qkv, plane)
    qkv_parts = layout.scatter_far(grad_qkv_part, got_qkv, later_qkv, plane)
    up_flip = layout.flip(up_sum, True)
    moved_output = layout.swap(output)
    one_other, qkv_parts, up_flip, moved_output, near_two_grad = hold(
        one_other, qkv_parts, up_flip, moved_output, near_two_grad
    )

    own_one_grad = one_part[:rows] + one_got[:rows].astype(F32) + one_other.astype(F32)
    norm_parts = [
        jnp.sum(own_one_grad * unit_one[:rows], axis=0),
        jnp.sum(own_one_grad, axis=0),
        jnp.sum(near_two_grad[:rows] * unit_two[:rows], axis=0),
        jnp.sum(near_two_grad[:rows], axis=0),
    ]
    input_grad = resid_grad[:rows] + norm_backward(own_one_grad, unit_one[:rows], inverse_one[:rows], ln1_gain)
    input_grad, norm_parts, qkv_parts = hold(input_grad.astype(BF16), jnp.stack(norm_parts), qkv_parts)
    moved_input = layout.swap(input_grad)
    norm_parts = layout.sum_quad(norm_parts)
    qkv_sum = layout.scatter_sum(qkv_parts)
    one_sum = jnp.concatenate([qkv_sum, grad_out_sum.reshape(qkv_sum.shape[0], -1)], axis=1)
    norm_parts, one_sum, moved_input = hold(norm_parts, one_sum, moved_input)
    down_own, down_other = layout.own_shards(down_sum, down_flip, c)
    first, second = jnp.split(one_sum, 2)
    one_own = layout.swap(jnp.where(p == 0, first, second))
    one_far = layout.swap_over_back(jnp.where(p == 0, second, first))
    norm_sums = layout.sum_quads(norm_parts)
    up_own, up_other = layout.own_shards(up_sum, up_flip, c)
    down_got, up_got = layout.core(down_other), layout.core(up_other)
    grad_down = jnp.where(p == c, down_own, down_got)
    grad_up = jnp.where(p == c, up_own, up_got)
    one_own, one_far, norm_sums, grad_down, grad_up = hold(one_own, one_far, norm_sums, grad_down, grad_up)
    lanes = lambda part: slice(part * part_width, (part + 1) * part_width)
    total_of = lambda part: one_own[:, lanes(part)].astype(F32) + one_far[:, lanes(part)].astype(F32)
    grad_qkv = jnp.stack([total_of(0), total_of(1), total_of(2)], axis=1)
    grad_out = total_of(3).reshape(w_out.shape)
    output, input_grad = moved_output, moved_input
    return (
        output,
        input_grad,
        norm_sums[0],
        norm_sums[1],
        grad_qkv.reshape(w_qkv.shape),
        grad_out,
        norm_sums[2],
        norm_sums[3],
        grad_up,
        grad_down,
    )


def solution(mesh):
    return jax.shard_map(
        on_device,
        mesh=mesh,
        in_specs=(
            P(("dp", "mp"), None),
            P(("dp", "mp"), None),
            P("dp", None),
            P("dp"),
            P(),
            P(),
            P("dp", None, "mp"),
            P(("mp", "dp"), None),
            P(),
            P(),
            P("dp", "mp"),
            P(("mp", "dp"), None),
        ),
        out_specs=(
            P(("dp", "mp"), None),
            P(("dp", "mp"), None),
            P(),
            P(),
            P("dp", None, "mp"),
            P(("mp", "dp"), None),
            P(),
            P(),
            P("dp", "mp"),
            P(("mp", "dp"), None),
        ),
        check_vma=False,
    )
```

```python
import functools
import math

import jax
import jax.numpy as jnp
from jax import lax
from jax.experimental import pallas as pl
from jax.experimental.pallas import tpu as pltpu
from jax.sharding import PartitionSpec as P

HDIM = 128
PREFIX0 = 768
WINDOW = 512
EPSILON = 1e-05
MASKED = -1e30
AXES = ("dp", "mp")
F32 = jnp.float32
BF16 = jnp.bfloat16


def norm_forward(values, norm_gain, norm_bias):
    center = values - jnp.mean(values, axis=-1, keepdims=True)
    inverse = lax.rsqrt(jnp.mean(center * center, axis=-1, keepdims=True) + EPSILON)
    normalized = center * inverse
    return (normalized * norm_gain + norm_bias, normalized, inverse)


def norm_backward(upstream, normalized, inverse, norm_gain):
    scaled = upstream * norm_gain
    return inverse * (
        scaled
        - jnp.mean(scaled, axis=-1, keepdims=True)
        - normalized * jnp.mean(scaled * normalized, axis=-1, keepdims=True)
    )


def gelu_back(pre_values, upstream):
    return jax.vjp(lambda pre_value: jax.nn.gelu(pre_value, approximate=True), pre_values)[1](
        upstream
    )[0]


def dot_nt(left, right):
    return lax.dot_general(left, right, (((1,), (1,)), ((), ())), preferred_element_type=F32)


def dot_tn(left, right):
    return lax.dot_general(left, right, (((0,), (0,)), ((), ())), preferred_element_type=F32)


def dot_nn(left, right):
    return lax.dot_general(left, right, (((1,), (0,)), ((), ())), preferred_element_type=F32)


def key_range(block, rows):
    first = max(0, block * rows - (WINDOW - 1)) // rows
    return first * rows, (block + 1) * rows


def attend_kernel(heads, slots, index_ref, proj_ref, cos_ref, sin_ref, start_ref, mixed_ref, q_ref, k_ref, v_ref, lse_ref):
    index = index_ref[0]
    total = proj_ref.shape[0]
    rows = total // slots
    width = heads * HDIM
    for slot in range(slots):
        here = slice(slot * rows, (slot + 1) * rows)
        there = pl.ds(pl.multiple_of((index ^ slot) * rows, rows), rows)
        cosine, sine = cos_ref[here, :], sin_ref[here, :]
        for head in range(heads):
            for part, out in enumerate((q_ref, k_ref)):
                lane = part * width + head * HDIM
                value = proj_ref[here, lane : lane + HDIM]
                value = value * cosine + pltpu.roll(value, HDIM // 2, 1) * sine
                out[head, there, :] = value.astype(BF16)
            lane = 2 * width + head * HDIM
            v_ref[head, there, :] = proj_ref[here, lane : lane + HDIM].astype(BF16)
    for block in range(slots):
        low, high = key_range(block, rows)
        here = slice(block * rows, (block + 1) * rows)
        slot_rows = pl.ds(pl.multiple_of((index ^ block) * rows, rows), rows)
        query_place = block * rows + lax.broadcasted_iota(jnp.int32, (rows, high - low), 0)
        key_place = low + lax.broadcasted_iota(jnp.int32, (rows, high - low), 1)
        allowed = (key_place >= start_ref[slot_rows, :]) & (key_place <= query_place)
        for head in range(heads):
            scores = dot_nt(q_ref[head, here, :], k_ref[head, low:high, :]) * (HDIM**-0.5)
            scores = jnp.where(allowed, scores, MASKED)
            top = jnp.max(scores, axis=-1, keepdims=True)
            weights = jnp.exp(scores - top)
            mass = jnp.sum(weights, axis=-1, keepdims=True)
            weights = (weights / mass).astype(BF16)
            mixed = dot_nn(weights, v_ref[head, low:high, :])
            mixed_ref[slot_rows, head * HDIM : (head + 1) * HDIM] = mixed.astype(BF16)
            lse_ref[head, here, :] = top + jnp.log(mass)


def attend_back_kernel(
    heads, slots, index_ref, grad_ref, q_ref, k_ref, v_ref, lse_ref, cos_ref, sin_ref, start_ref, out_ref, dk_ref, dv_ref
):
    index = index_ref[0]
    total = grad_ref.shape[0]
    rows = total // slots
    width = heads * HDIM
    scale = HDIM**-0.5
    dk_ref[...] = jnp.zeros_like(dk_ref)
    dv_ref[...] = jnp.zeros_like(dv_ref)
    for block in range(slots):
        low, high = key_range(block, rows)
        here = slice(block * rows, (block + 1) * rows)
        slot_rows = pl.ds(pl.multiple_of((index ^ block) * rows, rows), rows)
        query_place = block * rows + lax.broadcasted_iota(jnp.int32, (rows, high - low), 0)
        key_place = low + lax.broadcasted_iota(jnp.int32, (rows, high - low), 1)
        allowed = (key_place >= start_ref[slot_rows, :]) & (key_place <= query_place)
        cosine, sine = cos_ref[slot_rows, :], sin_ref[slot_rows, :]
        for head in range(heads):
            query = q_ref[head, here, :]
            keys = k_ref[head, low:high, :]
            values = v_ref[head, low:high, :]
            grad = grad_ref[slot_rows, head * HDIM : (head + 1) * HDIM]
            scores = jnp.where(allowed, dot_nt(query, keys) * scale, MASKED)
            probs = jnp.exp(scores - lse_ref[head, here, :])
            prob_grad = dot_nt(grad, values)
            mean = jnp.sum(probs * prob_grad, axis=-1, keepdims=True)
            score_grad = (probs * (prob_grad - mean)).astype(BF16)
            query_grad = dot_nn(score_grad, keys) * scale
            query_grad = query_grad * cosine - pltpu.roll(query_grad, HDIM // 2, 1) * sine
            out_ref[slot_rows, head * HDIM : (head + 1) * HDIM] = query_grad.astype(BF16)
            dk_ref[head, low:high, :] += dot_tn(score_grad, query)
            dv_ref[head, low:high, :] += dot_tn(probs.astype(BF16), grad)
    for slot in range(slots):
        here = slice(slot * rows, (slot + 1) * rows)
        there = pl.ds(pl.multiple_of((index ^ slot) * rows, rows), rows)
        cosine, sine = cos_ref[here, :], sin_ref[here, :]
        for head in range(heads):
            key_grad = dk_ref[head, there, :] * scale
            key_grad = key_grad * cosine - pltpu.roll(key_grad, HDIM // 2, 1) * sine
            lane = width + head * HDIM
            out_ref[here, lane : lane + HDIM] = key_grad.astype(BF16)
            lane = 2 * width + head * HDIM
            out_ref[here, lane : lane + HDIM] = dv_ref[head, there, :].astype(BF16)


def vmem():
    return pl.BlockSpec(memory_space=pltpu.VMEM)


def attend(index, proj, cosine, sine, start, heads, slots):
    total = proj.shape[0]
    shape = jax.ShapeDtypeStruct
    return pl.pallas_call(
        functools.partial(attend_kernel, heads, slots),
        in_specs=[pl.BlockSpec(memory_space=pltpu.SMEM)] + [vmem()] * 4,
        out_specs=[vmem()] * 5,
        out_shape=[
            shape((total, heads * HDIM), BF16),
            shape((heads, total, HDIM), BF16),
            shape((heads, total, HDIM), BF16),
            shape((heads, total, HDIM), BF16),
            shape((heads, total, 1), F32),
        ],
        cost_estimate=pl.CostEstimate(flops=3 * 10**9, bytes_accessed=12 * 10**6, transcendentals=2 * 10**6),
        name="attend",
    )(index, proj, cosine, sine, start)


def attend_back(index, grad, q, k, v, lse, cosine, sine, start, heads, slots):
    total = grad.shape[0]
    return pl.pallas_call(
        functools.partial(attend_back_kernel, heads, slots),
        in_specs=[pl.BlockSpec(memory_space=pltpu.SMEM)] + [vmem()] * 8,
        out_specs=vmem(),
        out_shape=jax.ShapeDtypeStruct((total, 3 * heads * HDIM), BF16),
        scratch_shapes=[pltpu.VMEM((heads, total, HDIM), F32)] * 2,
        cost_estimate=pl.CostEstimate(flops=6 * 10**9, bytes_accessed=12 * 10**6, transcendentals=2 * 10**6),
        name="attend_back",
    )(index, grad, q, k, v, lse, cosine, sine, start)


class Layout:
    def __init__(self, dp_count, mp_count):
        self.dp_count, self.mp_count = dp_count, mp_count
        self.planes = dp_count // 2
        self.groups = [[2 * plane + c for plane in range(self.planes)] for c in range(2)]

    def permute(self, value, place):
        pairs = []
        for plane in range(self.planes):
            for c in range(2):
                for p in range(2):
                    for zl in range(2):
                        target = place(plane, c, p, zl)
                        pairs.append((self.number(plane, c, p, zl), self.number(*target)))
        return lax.ppermute(value, AXES, pairs)

    def number(self, plane, c, p, zl):
        return (2 * plane + c) * self.mp_count + 2 * p + zl

    def swap(self, value):
        return self.permute(value, lambda plane, c, p, zl: (plane, p, c, zl))

    def swap_over(self, value):
        return self.permute(value, lambda plane, c, p, zl: (plane, p, 1 - c, zl))

    def send_shard(self, shard):
        return self.swap(shard), self.swap_over(shard)

    def line_up(self, shards, p):
        one, two = shards
        return jnp.where(p == 0, jnp.concatenate([one, two]), jnp.concatenate([two, one]))

    def sum_quad(self, value):
        value = value + self.core(value)
        return value + self.pair(value)

    def sum_quads(self, value):
        value = value + self.permute(value, lambda plane, c, p, zl: (plane, c, 1 - p, zl))
        step = 1
        while step < self.planes:
            value = value + self.plane_step(value, step)
            step *= 2
        return value

    def swap_over_back(self, value):
        return self.permute(value, lambda plane, c, p, zl: (plane, 1 - p, c, zl))

    def flip(self, value, into):
        pairs = []
        for plane in range(self.planes):
            for c in range(2):
                for zl in range(2):
                    near, far = self.number(plane, c, c, zl), self.number(plane, c, 1 - c, zl)
                    pairs.append((far, near) if into else (near, far))
        return lax.ppermute(value, AXES, pairs)

    def core(self, value):
        return self.permute(value, lambda plane, c, p, zl: (plane, 1 - c, p, zl))

    def pair(self, value):
        return self.permute(value, lambda plane, c, p, zl: (plane, c, p, 1 - zl))

    def plane_step(self, value, flip):
        return self.permute(value, lambda plane, c, p, zl: (plane ^ flip, c, p, zl))

    def both(self, shard, other, c):
        return jnp.where(c == 0, jnp.concatenate([shard, other]), jnp.concatenate([other, shard]))

    def gather(self, block):
        return lax.all_gather(block, "dp", axis=0, tiled=True, axis_index_groups=self.groups)

    def gather_near(self, block):
        if self.planes != 4:
            return (self.gather(block),)
        return block, self.plane_step(block, 1), self.plane_step(block, 2)

    def far_sends(self, pieces):
        if self.planes != 4:
            return ()
        half = pieces[0].shape[0] // 2
        return pieces[1][:half], pieces[2][half:]

    def gather_far(self, pieces, sends):
        if self.planes != 4:
            return pieces
        return *pieces, self.plane_step(sends[0], 2), self.plane_step(sends[1], 1)

    def assemble(self, pieces, plane):
        if self.planes != 4:
            return pieces[0]
        block, across, along, far_one, far_two = pieces
        rows = block.shape[0]
        whole = jnp.zeros((4 * rows, block.shape[1]), block.dtype)
        put = lambda whole, piece, place: lax.dynamic_update_slice(whole, piece, (place, 0))
        whole = put(whole, block, plane * rows)
        whole = put(whole, across, (plane ^ 1) * rows)
        whole = put(whole, along, (plane ^ 2) * rows)
        whole = put(whole, far_one, (plane ^ 3) * rows)
        return put(whole, far_two, (plane ^ 3) * rows + rows // 2)

    def scatter(self, grad):
        return lax.psum_scatter(grad, "dp", scatter_dimension=0, tiled=True, axis_index_groups=self.groups)

    def near_sends(self, grad, plane):
        if self.planes != 4:
            return ()
        rows = grad.shape[0] // 4
        half = rows // 2
        take = lambda place: lax.dynamic_slice(grad, (place, 0), (half, grad.shape[1]))
        return take((plane ^ 3) * rows), take((plane ^ 3) * rows + half)

    def scatter_near(self, grad, sends):
        if self.planes != 4:
            return self.scatter(grad)
        return self.plane_step(sends[0], 1), self.plane_step(sends[1], 2)

    def later_sends(self, grad, got, plane):
        if self.planes != 4:
            return ()
        rows = grad.shape[0] // 4
        half = rows // 2
        take = lambda place, count: lax.dynamic_slice(grad, (place, 0), (count, grad.shape[1]))
        add = lambda left, right: (left.astype(F32) + right.astype(F32)).astype(BF16)
        to_across = jnp.concatenate(
            [take((plane ^ 1) * rows, half), add(take((plane ^ 1) * rows + half, half), got[1])]
        )
        to_along = jnp.concatenate(
            [add(take((plane ^ 2) * rows, half), got[0]), take((plane ^ 2) * rows + half, half)]
        )
        return to_across, to_along

    def scatter_far(self, grad, got, sends, plane):
        if self.planes != 4:
            return got
        rows = grad.shape[0] // 4
        mine = lax.dynamic_slice(grad, (plane * rows, 0), (rows, grad.shape[1]))
        return mine, self.plane_step(sends[0], 1), self.plane_step(sends[1], 2)

    def scatter_sum(self, parts):
        if self.planes != 4:
            return parts
        return sum([part.astype(F32) for part in parts]).astype(BF16)

    def own_shards(self, part, received, c):
        whole = part.astype(F32) + received.astype(F32)
        first, second = jnp.split(whole, 2)
        return jnp.where(c == 0, first, second), jnp.where(c == 0, second, first)


def hold(*values):
    return lax.optimization_barrier(values)


def after(value, *others):
    return lax.optimization_barrier((value, others))[0]


def on_device(
    tokens,
    cotangent,
    lengths,
    granularity,
    ln1_gain,
    ln1_bias,
    w_qkv,
    w_out,
    ln2_gain,
    ln2_bias,
    w_up,
    w_down,
):
    layout = Layout(lax.axis_size("dp"), lax.axis_size("mp"))
    slots = 4
    dp_index, mp_index = lax.axis_index("dp"), lax.axis_index("mp")
    c, p, zl = dp_index % 2, mp_index // 2, mp_index % 2
    plane = dp_index // 2
    index = 2 * c + zl
    rows = tokens.shape[0]
    total = slots * rows
    part_width = w_qkv.shape[2]
    heads = part_width // HDIM
    units = w_up.shape[1]

    facts = jnp.concatenate([lengths[0], granularity])
    other_facts = layout.core(facts)
    facts = jnp.where(p == c, facts, other_facts)
    piece_lengths, piece_gran = facts[:-1], facts[-1]

    depth = w_qkv.shape[0]
    w_qkv_flat, _ = hold(w_qkv.reshape(depth, -1), other_facts)
    sent_qkv = layout.send_shard(w_qkv_flat)
    block_qkv = layout.line_up(sent_qkv, p)
    wide_qkv = layout.gather(block_qkv)
    moved_tokens = layout.swap(after(tokens, block_qkv))
    sent_out = layout.send_shard(after(w_out, block_qkv))
    other_down = layout.core(after(w_down, block_qkv))
    both_down = layout.both(w_down, other_down, c)

    slot_of = jnp.arange(total, dtype=jnp.int32) // rows
    places = (slot_of ^ index) * rows + jnp.arange(total, dtype=jnp.int32) % rows
    seg_ends = jnp.cumsum(piece_lengths)
    starts = seg_ends - piece_lengths
    seg_ids = jnp.sum((places[:, None] >= seg_ends[None, :]).astype(jnp.int32), axis=1)
    member = seg_ids[:, None] == jnp.arange(piece_lengths.shape[0], dtype=jnp.int32)[None, :]
    start = jnp.sum(jnp.where(member, starts[None, :], 0), axis=1)
    half = HDIM // 2
    frequencies = jnp.exp(jnp.arange(half, dtype=F32) * (-2.0 * math.log(10000.0) / HDIM))
    angles = (places - start).astype(F32)[:, None] * frequencies[None, :]
    cosine, sine = jnp.cos(angles), jnp.sin(angles)
    cosine = jnp.concatenate([cosine, cosine], axis=1)
    sine = jnp.concatenate([-sine, sine], axis=1)
    start = start[:, None]
    where = index[None]

    moved_tokens, cosine, sine, start, both_down = hold(moved_tokens, cosine, sine, start, both_down)
    pair_tokens = layout.pair(moved_tokens)
    block_out = layout.line_up(after(sent_out, moved_tokens), p)
    wide_out = layout.gather(block_out)
    pair_tokens, block_out = hold(pair_tokens, block_out)
    near_tokens = jnp.concatenate([moved_tokens, pair_tokens]).astype(F32)
    near_one, unit_one, inverse_one = norm_forward(near_tokens, ln1_gain, ln1_bias)
    near_one, w_up = hold(near_one.astype(BF16), w_up)
    sent_up = layout.send_shard(w_up)
    inputs_one = jnp.concatenate([near_one, layout.core(near_one)])
    projected = dot_nn(inputs_one, wide_qkv)
    projected, sent_up, both_down = hold(projected, sent_up, both_down)
    block_up, projected, both_down = hold(layout.line_up(sent_up, p), projected, both_down)
    pieces_up = layout.gather_near(block_up)
    flip_down = layout.flip(both_down, False)
    mixed, q_all, k_all, v_all, lse = attend(where, projected, cosine, sine, start, heads, slots)
    attn_part = dot_nn(mixed, wide_out)
    attn_send = attn_part[2 * rows :].astype(BF16)
    attn_send, pieces_up, flip_down = hold(attn_send, pieces_up, flip_down)

    attn_got, pieces_up, flip_down = hold(layout.core(attn_send), pieces_up, flip_down)
    attn_chip = attn_part[: 2 * rows] + attn_got.astype(F32)
    attn_low, pieces_up, flip_down, cotangent = hold(attn_chip.astype(BF16), pieces_up, flip_down, cotangent)
    attn_other = layout.pair(attn_low)
    block_down = jnp.where(p == c, both_down, flip_down)
    wide_down = layout.gather(block_down)
    pieces_up = layout.gather_far(pieces_up, layout.far_sends(pieces_up))
    moved_cot = layout.swap(cotangent)
    attn_other, pieces_up, moved_cot, block_down = hold(attn_other, pieces_up, moved_cot, block_down)

    def pair_order(other):
        other = other.astype(F32)
        return jnp.concatenate([other[rows:], other[:rows]])

    resid_one = near_tokens + attn_chip + pair_order(attn_other)
    near_two, unit_two, inverse_two = norm_forward(resid_one, ln2_gain, ln2_bias)
    near_two, pieces_up, moved_cot = hold(near_two.astype(BF16), pieces_up, moved_cot)
    pair_cot = layout.pair(moved_cot)
    inputs_two = jnp.concatenate([near_two, layout.core(near_two)])
    wide_up = layout.assemble(pieces_up, plane)

    prefix = PREFIX0 * jnp.left_shift(jnp.int32(1), piece_gran)
    active_units = jnp.clip(prefix - index * units, 0, units)
    keep_units = (jnp.arange(units, dtype=jnp.int32) < active_units).astype(F32)
    pre_act = dot_nn(inputs_two, wide_up)
    hidden_act = (jax.nn.gelu(pre_act, approximate=True) * keep_units).astype(BF16)
    hidden_act, pair_cot = hold(hidden_act, pair_cot)
    near_cot = jnp.concatenate([moved_cot, pair_cot])
    cot_all = jnp.concatenate([near_cot, layout.core(near_cot)])
    grad_down_part = dot_tn(hidden_act, cot_all).astype(BF16)
    grad_down_sum = layout.scatter(grad_down_part)
    wide_down = after(wide_down, grad_down_part)
    hidden_grad = dot_nt(cot_all, wide_down)
    pre_grad = (gelu_back(pre_act, hidden_grad) * keep_units).astype(BF16)
    ffn_part = dot_nt(pre_grad, wide_up)
    (ffn_send,) = hold(ffn_part[2 * rows :].astype(BF16))
    (ffn_got,) = hold(layout.core(ffn_send))
    ffn_chip = ffn_part[: 2 * rows] + ffn_got.astype(F32)
    ffn_low, pre_grad, hidden_act = hold(ffn_chip.astype(BF16), pre_grad, hidden_act)
    ffn_other = layout.pair(ffn_low)
    grad_up_part = dot_tn(inputs_two, pre_grad).astype(BF16)
    grad_up_sum = layout.scatter(grad_up_part)
    out_part = dot_nn(hidden_act, wide_down)
    out_send = out_part[2 * rows :].astype(BF16)
    ffn_other, out_send, grad_up_part = hold(ffn_other, out_send, grad_up_part)
    near_two_grad = ffn_chip + pair_order(ffn_other)

    resid_grad = near_cot.astype(F32) + norm_backward(near_two_grad, unit_two, inverse_two, ln2_gain)
    resid_low = resid_grad.astype(BF16)
    resid_low, out_send, down_sum = hold(resid_low, out_send, grad_down_sum)
    down_flip = layout.flip(down_sum, True)
    out_got = layout.core(out_send)
    resid_all = jnp.concatenate([resid_low, layout.core(resid_low)])
    mixed_grad = dot_nt(resid_all, wide_out).astype(BF16)
    grad_out_part = dot_tn(mixed, resid_all).astype(BF16)
    grad_out_sum = layout.scatter(grad_out_part)
    out_got = after(out_got, grad_out_part)
    out_send = (out_part[rows : 2 * rows] + out_got[rows:].astype(F32)).astype(BF16)
    out_other = layout.pair(out_send)
    projected_grad = attend_back(
        where, after(mixed_grad, out_send), q_all, k_all, v_all, lse, cosine, sine, start, heads, slots
    )
    grad_qkv_part = dot_tn(inputs_one, projected_grad).astype(BF16)
    near_qkv = layout.near_sends(grad_qkv_part, plane)
    near_qkv, down_flip, out_other, projected_grad = hold(near_qkv, down_flip, out_other, projected_grad)

    got_qkv = layout.scatter_near(grad_qkv_part, near_qkv)
    one_part = dot_nt(projected_grad, wide_qkv)
    output = resid_one[:rows] + out_part[:rows] + out_got[:rows].astype(F32) + out_other.astype(F32)
    one_send, got_qkv, output = hold(one_part[2 * rows :].astype(BF16), got_qkv, output.astype(BF16))
    (one_got,) = hold(layout.core(one_send))
    one_send = (one_part[rows : 2 * rows] + one_got[rows:].astype(F32)).astype(BF16)
    one_send, got_qkv, output, near_two_grad, up_sum = hold(one_send, got_qkv, output, near_two_grad, grad_up_sum)
    one_other = layout.pair(one_send)
    later_qkv = layout.later_sends(grad_qkv_part, got_qkv, plane)
    qkv_parts = layout.scatter_far(grad_qkv_part, got_qkv, later_qkv, plane)
    up_flip = layout.flip(up_sum, True)
    moved_output = layout.swap(output)
    one_other, qkv_parts, up_flip, moved_output, near_two_grad = hold(
        one_other, qkv_parts, up_flip, moved_output, near_two_grad
    )

    own_one_grad = one_part[:rows] + one_got[:rows].astype(F32) + one_other.astype(F32)
    norm_parts = [
        jnp.sum(own_one_grad * unit_one[:rows], axis=0),
        jnp.sum(own_one_grad, axis=0),
        jnp.sum(near_two_grad[:rows] * unit_two[:rows], axis=0),
        jnp.sum(near_two_grad[:rows], axis=0),
    ]
    input_grad = resid_grad[:rows] + norm_backward(own_one_grad, unit_one[:rows], inverse_one[:rows], ln1_gain)
    input_grad, norm_parts, qkv_parts = hold(input_grad.astype(BF16), jnp.stack(norm_parts), qkv_parts)
    moved_input = layout.swap(input_grad)
    norm_parts = layout.sum_quad(norm_parts)
    qkv_sum = layout.scatter_sum(qkv_parts)
    one_sum = jnp.concatenate([qkv_sum, grad_out_sum.reshape(qkv_sum.shape[0], -1)], axis=1)
    norm_parts, one_sum, moved_input = hold(norm_parts, one_sum, moved_input)
    down_own, down_other = layout.own_shards(down_sum, down_flip, c)
    first, second = jnp.split(one_sum, 2)
    one_own = layout.swap(jnp.where(p == 0, first, second))
    one_far = layout.swap_over_back(jnp.where(p == 0, second, first))
    norm_sums = layout.sum_quads(norm_parts)
    up_own, up_other = layout.own_shards(up_sum, up_flip, c)
    down_got, up_got = layout.core(down_other), layout.core(up_other)
    grad_down = jnp.where(p == c, down_own, down_got)
    grad_up = jnp.where(p == c, up_own, up_got)
    one_own, one_far, norm_sums, grad_down, grad_up = hold(one_own, one_far, norm_sums, grad_down, grad_up)
    lanes = lambda part: slice(part * part_width, (part + 1) * part_width)
    total_of = lambda part: one_own[:, lanes(part)].astype(F32) + one_far[:, lanes(part)].astype(F32)
    grad_qkv = jnp.stack([total_of(0), total_of(1), total_of(2)], axis=1)
    grad_out = total_of(3).reshape(w_out.shape)
    output, input_grad = moved_output, moved_input
    return (
        output,
        input_grad,
        norm_sums[0],
        norm_sums[1],
        grad_qkv.reshape(w_qkv.shape),
        grad_out,
        norm_sums[2],
        norm_sums[3],
        grad_up,
        grad_down,
    )


def solution(mesh):
    return jax.shard_map(
        on_device,
        mesh=mesh,
        in_specs=(
            P(("dp", "mp"), None),
            P(("dp", "mp"), None),
            P("dp", None),
            P("dp"),
            P(),
            P(),
            P("dp", None, "mp"),
            P(("mp", "dp"), None),
            P(),
            P(),
            P("dp", "mp"),
            P(("mp", "dp"), None),
        ),
        out_specs=(
            P(("dp", "mp"), None),
            P(("dp", "mp"), None),
            P(),
            P(),
            P("dp", None, "mp"),
            P(("mp", "dp"), None),
            P(),
            P(),
            P("dp", "mp"),
            P(("mp", "dp"), None),
        ),
        check_vma=False,
    )
```

```python
import functools
import math

import jax
import jax.numpy as jnp
from jax import lax
from jax.experimental import pallas as pl
from jax.experimental.pallas import tpu as pltpu
from jax.sharding import PartitionSpec as P

HDIM = 128
PREFIX0 = 768
WINDOW = 512
EPSILON = 1e-05
MASKED = -1e30
AXES = ("dp", "mp")
F32 = jnp.float32
BF16 = jnp.bfloat16


def norm_forward(values, norm_gain, norm_bias):
    center = values - jnp.mean(values, axis=-1, keepdims=True)
    inverse = lax.rsqrt(jnp.mean(center * center, axis=-1, keepdims=True) + EPSILON)
    normalized = center * inverse
    return (normalized * norm_gain + norm_bias, normalized, inverse)


def norm_backward(upstream, normalized, inverse, norm_gain):
    scaled = upstream * norm_gain
    return inverse * (
        scaled
        - jnp.mean(scaled, axis=-1, keepdims=True)
        - normalized * jnp.mean(scaled * normalized, axis=-1, keepdims=True)
    )


def gelu_back(pre_values, upstream):
    return jax.vjp(lambda pre_value: jax.nn.gelu(pre_value, approximate=True), pre_values)[1](
        upstream
    )[0]


def dot_nt(left, right):
    return lax.dot_general(left, right, (((1,), (1,)), ((), ())), preferred_element_type=F32)


def dot_tn(left, right):
    return lax.dot_general(left, right, (((0,), (0,)), ((), ())), preferred_element_type=F32)


def dot_nn(left, right):
    return lax.dot_general(left, right, (((1,), (0,)), ((), ())), preferred_element_type=F32)


def key_range(block, rows):
    first = max(0, block * rows - (WINDOW - 1)) // rows
    return first * rows, (block + 1) * rows


def attend_kernel(heads, slots, index_ref, proj_ref, cos_ref, sin_ref, start_ref, mixed_ref, q_ref, k_ref, v_ref, lse_ref):
    index = index_ref[0]
    total = proj_ref.shape[0]
    rows = total // slots
    width = heads * HDIM
    for slot in range(slots):
        here = slice(slot * rows, (slot + 1) * rows)
        there = pl.ds(pl.multiple_of((index ^ slot) * rows, rows), rows)
        cosine, sine = cos_ref[here, :], sin_ref[here, :]
        for head in range(heads):
            for part, out in enumerate((q_ref, k_ref)):
                lane = part * width + head * HDIM
                value = proj_ref[here, lane : lane + HDIM]
                value = value * cosine + pltpu.roll(value, HDIM // 2, 1) * sine
                out[head, there, :] = value.astype(BF16)
            lane = 2 * width + head * HDIM
            v_ref[head, there, :] = proj_ref[here, lane : lane + HDIM].astype(BF16)
    for block in range(slots):
        low, high = key_range(block, rows)
        here = slice(block * rows, (block + 1) * rows)
        slot_rows = pl.ds(pl.multiple_of((index ^ block) * rows, rows), rows)
        query_place = block * rows + lax.broadcasted_iota(jnp.int32, (rows, high - low), 0)
        key_place = low + lax.broadcasted_iota(jnp.int32, (rows, high - low), 1)
        allowed = (key_place >= start_ref[slot_rows, :]) & (key_place <= query_place)
        for head in range(heads):
            scores = dot_nt(q_ref[head, here, :], k_ref[head, low:high, :]) * (HDIM**-0.5)
            scores = jnp.where(allowed, scores, MASKED)
            top = jnp.max(scores, axis=-1, keepdims=True)
            weights = jnp.exp(scores - top)
            mass = jnp.sum(weights, axis=-1, keepdims=True)
            weights = (weights / mass).astype(BF16)
            mixed = dot_nn(weights, v_ref[head, low:high, :])
            mixed_ref[slot_rows, head * HDIM : (head + 1) * HDIM] = mixed.astype(BF16)
            lse_ref[head, here, :] = top + jnp.log(mass)


def attend_back_kernel(
    heads, slots, index_ref, grad_ref, q_ref, k_ref, v_ref, lse_ref, cos_ref, sin_ref, start_ref, out_ref, dk_ref, dv_ref
):
    index = index_ref[0]
    total = grad_ref.shape[0]
    rows = total // slots
    width = heads * HDIM
    scale = HDIM**-0.5
    dk_ref[...] = jnp.zeros_like(dk_ref)
    dv_ref[...] = jnp.zeros_like(dv_ref)
    for block in range(slots):
        low, high = key_range(block, rows)
        here = slice(block * rows, (block + 1) * rows)
        slot_rows = pl.ds(pl.multiple_of((index ^ block) * rows, rows), rows)
        query_place = block * rows + lax.broadcasted_iota(jnp.int32, (rows, high - low), 0)
        key_place = low + lax.broadcasted_iota(jnp.int32, (rows, high - low), 1)
        allowed = (key_place >= start_ref[slot_rows, :]) & (key_place <= query_place)
        cosine, sine = cos_ref[slot_rows, :], sin_ref[slot_rows, :]
        for head in range(heads):
            query = q_ref[head, here, :]
            keys = k_ref[head, low:high, :]
            values = v_ref[head, low:high, :]
            grad = grad_ref[slot_rows, head * HDIM : (head + 1) * HDIM]
            scores = jnp.where(allowed, dot_nt(query, keys) * scale, MASKED)
            probs = jnp.exp(scores - lse_ref[head, here, :])
            prob_grad = dot_nt(grad, values)
            mean = jnp.sum(probs * prob_grad, axis=-1, keepdims=True)
            score_grad = (probs * (prob_grad - mean)).astype(BF16)
            query_grad = dot_nn(score_grad, keys) * scale
            query_grad = query_grad * cosine - pltpu.roll(query_grad, HDIM // 2, 1) * sine
            out_ref[slot_rows, head * HDIM : (head + 1) * HDIM] = query_grad.astype(BF16)
            dk_ref[head, low:high, :] += dot_tn(score_grad, query)
            dv_ref[head, low:high, :] += dot_tn(probs.astype(BF16), grad)
    for slot in range(slots):
        here = slice(slot * rows, (slot + 1) * rows)
        there = pl.ds(pl.multiple_of((index ^ slot) * rows, rows), rows)
        cosine, sine = cos_ref[here, :], sin_ref[here, :]
        for head in range(heads):
            key_grad = dk_ref[head, there, :] * scale
            key_grad = key_grad * cosine - pltpu.roll(key_grad, HDIM // 2, 1) * sine
            lane = width + head * HDIM
            out_ref[here, lane : lane + HDIM] = key_grad.astype(BF16)
            lane = 2 * width + head * HDIM
            out_ref[here, lane : lane + HDIM] = dv_ref[head, there, :].astype(BF16)


def vmem():
    return pl.BlockSpec(memory_space=pltpu.VMEM)


def attend(index, proj, cosine, sine, start, heads, slots):
    total = proj.shape[0]
    shape = jax.ShapeDtypeStruct
    return pl.pallas_call(
        functools.partial(attend_kernel, heads, slots),
        in_specs=[pl.BlockSpec(memory_space=pltpu.SMEM)] + [vmem()] * 4,
        out_specs=[vmem()] * 5,
        out_shape=[
            shape((total, heads * HDIM), BF16),
            shape((heads, total, HDIM), BF16),
            shape((heads, total, HDIM), BF16),
            shape((heads, total, HDIM), BF16),
            shape((heads, total, 1), F32),
        ],
        cost_estimate=pl.CostEstimate(flops=3 * 10**9, bytes_accessed=12 * 10**6, transcendentals=2 * 10**6),
        name="attend",
    )(index, proj, cosine, sine, start)


def attend_back(index, grad, q, k, v, lse, cosine, sine, start, heads, slots):
    total = grad.shape[0]
    return pl.pallas_call(
        functools.partial(attend_back_kernel, heads, slots),
        in_specs=[pl.BlockSpec(memory_space=pltpu.SMEM)] + [vmem()] * 8,
        out_specs=vmem(),
        out_shape=jax.ShapeDtypeStruct((total, 3 * heads * HDIM), BF16),
        scratch_shapes=[pltpu.VMEM((heads, total, HDIM), F32)] * 2,
        cost_estimate=pl.CostEstimate(flops=6 * 10**9, bytes_accessed=12 * 10**6, transcendentals=2 * 10**6),
        name="attend_back",
    )(index, grad, q, k, v, lse, cosine, sine, start)


class Layout:
    def __init__(self, dp_count, mp_count):
        self.dp_count, self.mp_count = dp_count, mp_count
        self.planes = dp_count // 2
        self.groups = [[2 * plane + c for plane in range(self.planes)] for c in range(2)]

    def permute(self, value, place):
        pairs = []
        for plane in range(self.planes):
            for c in range(2):
                for p in range(2):
                    for zl in range(2):
                        target = place(plane, c, p, zl)
                        pairs.append((self.number(plane, c, p, zl), self.number(*target)))
        return lax.ppermute(value, AXES, pairs)

    def number(self, plane, c, p, zl):
        return (2 * plane + c) * self.mp_count + 2 * p + zl

    def swap(self, value):
        return self.permute(value, lambda plane, c, p, zl: (plane, p, c, zl))

    def swap_over(self, value):
        return self.permute(value, lambda plane, c, p, zl: (plane, p, 1 - c, zl))

    def send_shard(self, shard):
        return self.swap(shard), self.swap_over(shard)

    def line_up(self, shards, p):
        one, two = shards
        return jnp.where(p == 0, jnp.concatenate([one, two]), jnp.concatenate([two, one]))

    def sum_quad(self, value):
        value = value + self.core(value)
        return value + self.pair(value)

    def sum_quads(self, value):
        value = value + self.permute(value, lambda plane, c, p, zl: (plane, c, 1 - p, zl))
        step = 1
        while step < self.planes:
            value = value + self.plane_step(value, step)
            step *= 2
        return value

    def swap_over_back(self, value):
        return self.permute(value, lambda plane, c, p, zl: (plane, 1 - p, c, zl))

    def flip(self, value, into):
        pairs = []
        for plane in range(self.planes):
            for c in range(2):
                for zl in range(2):
                    near, far = self.number(plane, c, c, zl), self.number(plane, c, 1 - c, zl)
                    pairs.append((far, near) if into else (near, far))
        return lax.ppermute(value, AXES, pairs)

    def core(self, value):
        return self.permute(value, lambda plane, c, p, zl: (plane, 1 - c, p, zl))

    def pair(self, value):
        return self.permute(value, lambda plane, c, p, zl: (plane, c, p, 1 - zl))

    def plane_step(self, value, flip):
        return self.permute(value, lambda plane, c, p, zl: (plane ^ flip, c, p, zl))

    def both(self, shard, other, c):
        return jnp.where(c == 0, jnp.concatenate([shard, other]), jnp.concatenate([other, shard]))

    def gather(self, block):
        return lax.all_gather(block, "dp", axis=0, tiled=True, axis_index_groups=self.groups)

    def gather_near(self, block):
        if self.planes != 4:
            return (self.gather(block),)
        return block, self.plane_step(block, 1), self.plane_step(block, 2)

    def far_sends(self, pieces):
        if self.planes != 4:
            return ()
        half = pieces[0].shape[0] // 2
        return pieces[1][:half], pieces[2][half:]

    def gather_far(self, pieces, sends):
        if self.planes != 4:
            return pieces
        return *pieces, self.plane_step(sends[0], 2), self.plane_step(sends[1], 1)

    def assemble(self, pieces, plane):
        if self.planes != 4:
            return pieces[0]
        block, across, along, far_one, far_two = pieces
        rows = block.shape[0]
        whole = jnp.zeros((4 * rows, block.shape[1]), block.dtype)
        put = lambda whole, piece, place: lax.dynamic_update_slice(whole, piece, (place, 0))
        whole = put(whole, block, plane * rows)
        whole = put(whole, across, (plane ^ 1) * rows)
        whole = put(whole, along, (plane ^ 2) * rows)
        whole = put(whole, far_one, (plane ^ 3) * rows)
        return put(whole, far_two, (plane ^ 3) * rows + rows // 2)

    def scatter(self, grad):
        return lax.psum_scatter(grad, "dp", scatter_dimension=0, tiled=True, axis_index_groups=self.groups)

    def near_sends(self, grad, plane):
        if self.planes != 4:
            return ()
        rows = grad.shape[0] // 4
        half = rows // 2
        take = lambda place: lax.dynamic_slice(grad, (place, 0), (half, grad.shape[1]))
        return take((plane ^ 3) * rows), take((plane ^ 3) * rows + half)

    def scatter_near(self, grad, sends):
        if self.planes != 4:
            return self.scatter(grad)
        return self.plane_step(sends[0], 1), self.plane_step(sends[1], 2)

    def later_sends(self, grad, got, plane):
        if self.planes != 4:
            return ()
        rows = grad.shape[0] // 4
        half = rows // 2
        take = lambda place, count: lax.dynamic_slice(grad, (place, 0), (count, grad.shape[1]))
        add = lambda left, right: (left.astype(F32) + right.astype(F32)).astype(BF16)
        to_across = jnp.concatenate(
            [take((plane ^ 1) * rows, half), add(take((plane ^ 1) * rows + half, half), got[1])]
        )
        to_along = jnp.concatenate(
            [add(take((plane ^ 2) * rows, half), got[0]), take((plane ^ 2) * rows + half, half)]
        )
        return to_across, to_along

    def scatter_far(self, grad, got, sends, plane):
        if self.planes != 4:
            return got
        rows = grad.shape[0] // 4
        mine = lax.dynamic_slice(grad, (plane * rows, 0), (rows, grad.shape[1]))
        return mine, self.plane_step(sends[0], 1), self.plane_step(sends[1], 2)

    def scatter_sum(self, parts):
        if self.planes != 4:
            return parts
        return sum([part.astype(F32) for part in parts]).astype(BF16)

    def own_shards(self, part, received, c):
        whole = part.astype(F32) + received.astype(F32)
        first, second = jnp.split(whole, 2)
        return jnp.where(c == 0, first, second), jnp.where(c == 0, second, first)


def hold(*values):
    return lax.optimization_barrier(values)


def after(value, *others):
    return lax.optimization_barrier((value, others))[0]


def on_device(
    tokens,
    cotangent,
    lengths,
    granularity,
    ln1_gain,
    ln1_bias,
    w_qkv,
    w_out,
    ln2_gain,
    ln2_bias,
    w_up,
    w_down,
):
    layout = Layout(lax.axis_size("dp"), lax.axis_size("mp"))
    slots = 4
    dp_index, mp_index = lax.axis_index("dp"), lax.axis_index("mp")
    c, p, zl = dp_index % 2, mp_index // 2, mp_index % 2
    plane = dp_index // 2
    index = 2 * c + zl
    rows = tokens.shape[0]
    total = slots * rows
    part_width = w_qkv.shape[2]
    heads = part_width // HDIM
    units = w_up.shape[1]

    facts = jnp.concatenate([lengths[0], granularity])
    other_facts = layout.core(facts)
    facts = jnp.where(p == c, facts, other_facts)
    piece_lengths, piece_gran = facts[:-1], facts[-1]

    depth = w_qkv.shape[0]
    w_qkv_flat, _ = hold(w_qkv.reshape(depth, -1), other_facts)
    sent_qkv = layout.send_shard(w_qkv_flat)
    block_qkv = layout.line_up(sent_qkv, p)
    wide_qkv = layout.gather(block_qkv)
    moved_tokens = layout.swap(after(tokens, block_qkv))
    sent_out = layout.send_shard(after(w_out, block_qkv))
    other_down = layout.core(after(w_down, block_qkv))
    both_down = layout.both(w_down, other_down, c)

    slot_of = jnp.arange(total, dtype=jnp.int32) // rows
    places = (slot_of ^ index) * rows + jnp.arange(total, dtype=jnp.int32) % rows
    seg_ends = jnp.cumsum(piece_lengths)
    starts = seg_ends - piece_lengths
    seg_ids = jnp.sum((places[:, None] >= seg_ends[None, :]).astype(jnp.int32), axis=1)
    member = seg_ids[:, None] == jnp.arange(piece_lengths.shape[0], dtype=jnp.int32)[None, :]
    start = jnp.sum(jnp.where(member, starts[None, :], 0), axis=1)
    half = HDIM // 2
    frequencies = jnp.exp(jnp.arange(half, dtype=F32) * (-2.0 * math.log(10000.0) / HDIM))
    angles = (places - start).astype(F32)[:, None] * frequencies[None, :]
    cosine, sine = jnp.cos(angles), jnp.sin(angles)
    cosine = jnp.concatenate([cosine, cosine], axis=1)
    sine = jnp.concatenate([-sine, sine], axis=1)
    start = start[:, None]
    where = index[None]

    moved_tokens, cosine, sine, start, both_down = hold(moved_tokens, cosine, sine, start, both_down)
    pair_tokens = layout.pair(moved_tokens)
    block_out = layout.line_up(after(sent_out, moved_tokens), p)
    wide_out = layout.gather(block_out)
    pair_tokens, block_out = hold(pair_tokens, block_out)
    near_tokens = jnp.concatenate([moved_tokens, pair_tokens]).astype(F32)
    near_one, unit_one, inverse_one = norm_forward(near_tokens, ln1_gain, ln1_bias)
    near_one, w_up = hold(near_one.astype(BF16), w_up)
    sent_up = layout.send_shard(w_up)
    inputs_one = jnp.concatenate([near_one, layout.core(near_one)])
    projected = dot_nn(inputs_one, wide_qkv)
    projected, sent_up, both_down = hold(projected, sent_up, both_down)
    block_up, projected, both_down = hold(layout.line_up(sent_up, p), projected, both_down)
    pieces_up = layout.gather_near(block_up)
    flip_down = layout.flip(both_down, False)
    mixed, q_all, k_all, v_all, lse = attend(where, projected, cosine, sine, start, heads, slots)
    attn_part = dot_nn(mixed, wide_out)
    attn_send = attn_part[2 * rows :].astype(BF16)
    attn_send, pieces_up, flip_down = hold(attn_send, pieces_up, flip_down)

    attn_got, pieces_up, flip_down = hold(layout.core(attn_send), pieces_up, flip_down)
    attn_chip = attn_part[: 2 * rows] + attn_got.astype(F32)
    attn_low, pieces_up, flip_down, cotangent = hold(attn_chip.astype(BF16), pieces_up, flip_down, cotangent)
    attn_other = layout.pair(attn_low)
    block_down = jnp.where(p == c, both_down, flip_down)
    wide_down = layout.gather(block_down)
    pieces_up = layout.gather_far(pieces_up, layout.far_sends(pieces_up))
    moved_cot = layout.swap(cotangent)
    attn_other, pieces_up, moved_cot, block_down = hold(attn_other, pieces_up, moved_cot, block_down)

    def pair_order(other):
        other = other.astype(F32)
        return jnp.concatenate([other[rows:], other[:rows]])

    resid_one = near_tokens + attn_chip + pair_order(attn_other)
    near_two, unit_two, inverse_two = norm_forward(resid_one, ln2_gain, ln2_bias)
    near_two, pieces_up, moved_cot = hold(near_two.astype(BF16), pieces_up, moved_cot)
    pair_cot = layout.pair(moved_cot)
    inputs_two = jnp.concatenate([near_two, layout.core(near_two)])
    wide_up = layout.assemble(pieces_up, plane)

    prefix = PREFIX0 * jnp.left_shift(jnp.int32(1), piece_gran)
    active_units = jnp.clip(prefix - index * units, 0, units)
    keep_units = (jnp.arange(units, dtype=jnp.int32) < active_units).astype(F32)
    pre_act = dot_nn(inputs_two, wide_up)
    hidden_act = (jax.nn.gelu(pre_act, approximate=True) * keep_units).astype(BF16)
    hidden_act, pair_cot = hold(hidden_act, pair_cot)
    near_cot = jnp.concatenate([moved_cot, pair_cot])
    cot_all = jnp.concatenate([near_cot, layout.core(near_cot)])
    grad_down_part = dot_tn(hidden_act, cot_all).astype(BF16)
    grad_down_sum = layout.scatter(grad_down_part)
    wide_down = after(wide_down, grad_down_part)
    hidden_grad = dot_nt(cot_all, wide_down)
    pre_grad = (gelu_back(pre_act, hidden_grad) * keep_units).astype(BF16)
    ffn_part = dot_nt(pre_grad, wide_up)
    (ffn_send,) = hold(ffn_part[2 * rows :].astype(BF16))
    (ffn_got,) = hold(layout.core(ffn_send))
    ffn_chip = ffn_part[: 2 * rows] + ffn_got.astype(F32)
    ffn_low, pre_grad, hidden_act = hold(ffn_chip.astype(BF16), pre_grad, hidden_act)
    ffn_other = layout.pair(ffn_low)
    grad_up_part = dot_tn(inputs_two, pre_grad).astype(BF16)
    grad_up_sum = layout.scatter(grad_up_part)
    out_part = dot_nn(hidden_act, wide_down)
    out_send = out_part[2 * rows :].astype(BF16)
    ffn_other, out_send, grad_up_part = hold(ffn_other, out_send, grad_up_part)
    near_two_grad = ffn_chip + pair_order(ffn_other)

    resid_grad = near_cot.astype(F32) + norm_backward(near_two_grad, unit_two, inverse_two, ln2_gain)
    resid_low = resid_grad.astype(BF16)
    resid_low, out_send, down_sum = hold(resid_low, out_send, grad_down_sum)
    down_flip = layout.flip(down_sum, True)
    out_got = layout.core(out_send)
    resid_all = jnp.concatenate([resid_low, layout.core(resid_low)])
    mixed_grad = dot_nt(resid_all, wide_out).astype(BF16)
    grad_out_part = dot_tn(mixed, resid_all).astype(BF16)
    grad_out_sum = layout.scatter(grad_out_part)
    out_got = after(out_got, grad_out_part)
    out_send = (out_part[rows : 2 * rows] + out_got[rows:].astype(F32)).astype(BF16)
    out_other = layout.pair(out_send)
    projected_grad = attend_back(
        where, after(mixed_grad, out_send), q_all, k_all, v_all, lse, cosine, sine, start, heads, slots
    )
    grad_qkv_part = dot_tn(inputs_one, projected_grad).astype(BF16)
    near_qkv = layout.near_sends(grad_qkv_part, plane)
    near_qkv, down_flip, out_other, projected_grad = hold(near_qkv, down_flip, out_other, projected_grad)

    got_qkv = layout.scatter_near(grad_qkv_part, near_qkv)
    one_part = dot_nt(projected_grad, wide_qkv)
    one_send, got_qkv = hold(one_part[2 * rows :].astype(BF16), got_qkv)
    one_got = layout.core(one_send)
    output = resid_one[:rows] + out_part[:rows] + out_got[:rows].astype(F32) + after(out_other, one_send).astype(F32)
    one_got, output = hold(one_got, output.astype(BF16))
    one_send = (one_part[rows : 2 * rows] + one_got[rows:].astype(F32)).astype(BF16)
    one_send, got_qkv, output, near_two_grad, up_sum = hold(one_send, got_qkv, output, near_two_grad, grad_up_sum)
    one_other = layout.pair(one_send)
    later_qkv = layout.later_sends(grad_qkv_part, got_qkv, plane)
    qkv_parts = layout.scatter_far(grad_qkv_part, got_qkv, later_qkv, plane)
    up_flip = layout.flip(up_sum, True)
    moved_output = layout.swap(output)
    one_other, qkv_parts, up_flip, moved_output, near_two_grad = hold(
        one_other, qkv_parts, up_flip, moved_output, near_two_grad
    )

    own_one_grad = one_part[:rows] + one_got[:rows].astype(F32) + one_other.astype(F32)
    norm_parts = [
        jnp.sum(own_one_grad * unit_one[:rows], axis=0),
        jnp.sum(own_one_grad, axis=0),
        jnp.sum(near_two_grad[:rows] * unit_two[:rows], axis=0),
        jnp.sum(near_two_grad[:rows], axis=0),
    ]
    input_grad = resid_grad[:rows] + norm_backward(own_one_grad, unit_one[:rows], inverse_one[:rows], ln1_gain)
    input_grad, norm_parts, qkv_parts = hold(input_grad.astype(BF16), jnp.stack(norm_parts), qkv_parts)
    moved_input = layout.swap(input_grad)
    norm_parts = layout.sum_quad(norm_parts)
    qkv_sum = layout.scatter_sum(qkv_parts)
    one_sum = jnp.concatenate([qkv_sum, grad_out_sum.reshape(qkv_sum.shape[0], -1)], axis=1)
    norm_parts, one_sum, moved_input = hold(norm_parts, one_sum, moved_input)
    down_own, down_other = layout.own_shards(down_sum, down_flip, c)
    first, second = jnp.split(one_sum, 2)
    one_own = layout.swap(jnp.where(p == 0, first, second))
    one_far = layout.swap_over_back(jnp.where(p == 0, second, first))
    norm_sums = layout.sum_quads(norm_parts)
    up_own, up_other = layout.own_shards(up_sum, up_flip, c)
    down_got, up_got = layout.core(down_other), layout.core(up_other)
    grad_down = jnp.where(p == c, down_own, down_got)
    grad_up = jnp.where(p == c, up_own, up_got)
    one_own, one_far, norm_sums, grad_down, grad_up = hold(one_own, one_far, norm_sums, grad_down, grad_up)
    lanes = lambda part: slice(part * part_width, (part + 1) * part_width)
    total_of = lambda part: one_own[:, lanes(part)].astype(F32) + one_far[:, lanes(part)].astype(F32)
    grad_qkv = jnp.stack([total_of(0), total_of(1), total_of(2)], axis=1)
    grad_out = total_of(3).reshape(w_out.shape)
    output, input_grad = moved_output, moved_input
    return (
        output,
        input_grad,
        norm_sums[0],
        norm_sums[1],
        grad_qkv.reshape(w_qkv.shape),
        grad_out,
        norm_sums[2],
        norm_sums[3],
        grad_up,
        grad_down,
    )


def solution(mesh):
    return jax.shard_map(
        on_device,
        mesh=mesh,
        in_specs=(
            P(("dp", "mp"), None),
            P(("dp", "mp"), None),
            P("dp", None),
            P("dp"),
            P(),
            P(),
            P("dp", None, "mp"),
            P(("mp", "dp"), None),
            P(),
            P(),
            P("dp", "mp"),
            P(("mp", "dp"), None),
        ),
        out_specs=(
            P(("dp", "mp"), None),
            P(("dp", "mp"), None),
            P(),
            P(),
            P("dp", None, "mp"),
            P(("mp", "dp"), None),
            P(),
            P(),
            P("dp", "mp"),
            P(("mp", "dp"), None),
        ),
        check_vma=False,
    )
```

```python
import functools
import math

import jax
import jax.numpy as jnp
from jax import lax
from jax.experimental import pallas as pl
from jax.experimental.pallas import tpu as pltpu
from jax.sharding import PartitionSpec as P

HDIM = 128
PREFIX0 = 768
WINDOW = 512
EPSILON = 1e-05
MASKED = -1e30
AXES = ("dp", "mp")
F32 = jnp.float32
BF16 = jnp.bfloat16


def norm_forward(values, norm_gain, norm_bias):
    center = values - jnp.mean(values, axis=-1, keepdims=True)
    inverse = lax.rsqrt(jnp.mean(center * center, axis=-1, keepdims=True) + EPSILON)
    normalized = center * inverse
    return (normalized * norm_gain + norm_bias, normalized, inverse)


def norm_backward(upstream, normalized, inverse, norm_gain):
    scaled = upstream * norm_gain
    return inverse * (
        scaled
        - jnp.mean(scaled, axis=-1, keepdims=True)
        - normalized * jnp.mean(scaled * normalized, axis=-1, keepdims=True)
    )


def gelu_back(pre_values, upstream):
    return jax.vjp(lambda pre_value: jax.nn.gelu(pre_value, approximate=True), pre_values)[1](
        upstream
    )[0]


def dot_nt(left, right):
    return lax.dot_general(left, right, (((1,), (1,)), ((), ())), preferred_element_type=F32)


def dot_tn(left, right):
    return lax.dot_general(left, right, (((0,), (0,)), ((), ())), preferred_element_type=F32)


def dot_nn(left, right):
    return lax.dot_general(left, right, (((1,), (0,)), ((), ())), preferred_element_type=F32)


def key_range(block, rows):
    first = max(0, block * rows - (WINDOW - 1)) // rows
    return first * rows, (block + 1) * rows


def attend_kernel(heads, slots, index_ref, proj_ref, cos_ref, sin_ref, start_ref, mixed_ref, q_ref, k_ref, v_ref, lse_ref):
    index = index_ref[0]
    total = proj_ref.shape[0]
    rows = total // slots
    width = heads * HDIM
    for slot in range(slots):
        here = slice(slot * rows, (slot + 1) * rows)
        there = pl.ds(pl.multiple_of((index ^ slot) * rows, rows), rows)
        cosine, sine = cos_ref[here, :], sin_ref[here, :]
        for head in range(heads):
            for part, out in enumerate((q_ref, k_ref)):
                lane = part * width + head * HDIM
                value = proj_ref[here, lane : lane + HDIM]
                value = value * cosine + pltpu.roll(value, HDIM // 2, 1) * sine
                out[head, there, :] = value.astype(BF16)
            lane = 2 * width + head * HDIM
            v_ref[head, there, :] = proj_ref[here, lane : lane + HDIM].astype(BF16)
    for block in range(slots):
        low, high = key_range(block, rows)
        here = slice(block * rows, (block + 1) * rows)
        slot_rows = pl.ds(pl.multiple_of((index ^ block) * rows, rows), rows)
        query_place = block * rows + lax.broadcasted_iota(jnp.int32, (rows, high - low), 0)
        key_place = low + lax.broadcasted_iota(jnp.int32, (rows, high - low), 1)
        allowed = (key_place >= start_ref[slot_rows, :]) & (key_place <= query_place)
        for head in range(heads):
            scores = dot_nt(q_ref[head, here, :], k_ref[head, low:high, :]) * (HDIM**-0.5)
            scores = jnp.where(allowed, scores, MASKED)
            top = jnp.max(scores, axis=-1, keepdims=True)
            weights = jnp.exp(scores - top)
            mass = jnp.sum(weights, axis=-1, keepdims=True)
            weights = (weights / mass).astype(BF16)
            mixed = dot_nn(weights, v_ref[head, low:high, :])
            mixed_ref[slot_rows, head * HDIM : (head + 1) * HDIM] = mixed.astype(BF16)
            lse_ref[head, here, :] = top + jnp.log(mass)


def attend_back_kernel(
    heads, slots, index_ref, grad_ref, q_ref, k_ref, v_ref, lse_ref, cos_ref, sin_ref, start_ref, out_ref, dk_ref, dv_ref
):
    index = index_ref[0]
    total = grad_ref.shape[0]
    rows = total // slots
    width = heads * HDIM
    scale = HDIM**-0.5
    dk_ref[...] = jnp.zeros_like(dk_ref)
    dv_ref[...] = jnp.zeros_like(dv_ref)
    for block in range(slots):
        low, high = key_range(block, rows)
        here = slice(block * rows, (block + 1) * rows)
        slot_rows = pl.ds(pl.multiple_of((index ^ block) * rows, rows), rows)
        query_place = block * rows + lax.broadcasted_iota(jnp.int32, (rows, high - low), 0)
        key_place = low + lax.broadcasted_iota(jnp.int32, (rows, high - low), 1)
        allowed = (key_place >= start_ref[slot_rows, :]) & (key_place <= query_place)
        cosine, sine = cos_ref[slot_rows, :], sin_ref[slot_rows, :]
        for head in range(heads):
            query = q_ref[head, here, :]
            keys = k_ref[head, low:high, :]
            values = v_ref[head, low:high, :]
            grad = grad_ref[slot_rows, head * HDIM : (head + 1) * HDIM]
            scores = jnp.where(allowed, dot_nt(query, keys) * scale, MASKED)
            probs = jnp.exp(scores - lse_ref[head, here, :])
            prob_grad = dot_nt(grad, values)
            mean = jnp.sum(probs * prob_grad, axis=-1, keepdims=True)
            score_grad = (probs * (prob_grad - mean)).astype(BF16)
            query_grad = dot_nn(score_grad, keys) * scale
            query_grad = query_grad * cosine - pltpu.roll(query_grad, HDIM // 2, 1) * sine
            out_ref[slot_rows, head * HDIM : (head + 1) * HDIM] = query_grad.astype(BF16)
            dk_ref[head, low:high, :] += dot_tn(score_grad, query)
            dv_ref[head, low:high, :] += dot_tn(probs.astype(BF16), grad)
    for slot in range(slots):
        here = slice(slot * rows, (slot + 1) * rows)
        there = pl.ds(pl.multiple_of((index ^ slot) * rows, rows), rows)
        cosine, sine = cos_ref[here, :], sin_ref[here, :]
        for head in range(heads):
            key_grad = dk_ref[head, there, :] * scale
            key_grad = key_grad * cosine - pltpu.roll(key_grad, HDIM // 2, 1) * sine
            lane = width + head * HDIM
            out_ref[here, lane : lane + HDIM] = key_grad.astype(BF16)
            lane = 2 * width + head * HDIM
            out_ref[here, lane : lane + HDIM] = dv_ref[head, there, :].astype(BF16)


def vmem():
    return pl.BlockSpec(memory_space=pltpu.VMEM)


def attend(index, proj, cosine, sine, start, heads, slots):
    total = proj.shape[0]
    shape = jax.ShapeDtypeStruct
    return pl.pallas_call(
        functools.partial(attend_kernel, heads, slots),
        in_specs=[pl.BlockSpec(memory_space=pltpu.SMEM)] + [vmem()] * 4,
        out_specs=[vmem()] * 5,
        out_shape=[
            shape((total, heads * HDIM), BF16),
            shape((heads, total, HDIM), BF16),
            shape((heads, total, HDIM), BF16),
            shape((heads, total, HDIM), BF16),
            shape((heads, total, 1), F32),
        ],
        cost_estimate=pl.CostEstimate(flops=3 * 10**9, bytes_accessed=12 * 10**6, transcendentals=2 * 10**6),
        name="attend",
    )(index, proj, cosine, sine, start)


def attend_back(index, grad, q, k, v, lse, cosine, sine, start, heads, slots):
    total = grad.shape[0]
    return pl.pallas_call(
        functools.partial(attend_back_kernel, heads, slots),
        in_specs=[pl.BlockSpec(memory_space=pltpu.SMEM)] + [vmem()] * 8,
        out_specs=vmem(),
        out_shape=jax.ShapeDtypeStruct((total, 3 * heads * HDIM), BF16),
        scratch_shapes=[pltpu.VMEM((heads, total, HDIM), F32)] * 2,
        cost_estimate=pl.CostEstimate(flops=6 * 10**9, bytes_accessed=12 * 10**6, transcendentals=2 * 10**6),
        name="attend_back",
    )(index, grad, q, k, v, lse, cosine, sine, start)


class Layout:
    def __init__(self, dp_count, mp_count):
        self.dp_count, self.mp_count = dp_count, mp_count
        self.planes = dp_count // 2
        self.groups = [[2 * plane + c for plane in range(self.planes)] for c in range(2)]

    def permute(self, value, place):
        pairs = []
        for plane in range(self.planes):
            for c in range(2):
                for p in range(2):
                    for zl in range(2):
                        target = place(plane, c, p, zl)
                        pairs.append((self.number(plane, c, p, zl), self.number(*target)))
        return lax.ppermute(value, AXES, pairs)

    def number(self, plane, c, p, zl):
        return (2 * plane + c) * self.mp_count + 2 * p + zl

    def swap(self, value):
        return self.permute(value, lambda plane, c, p, zl: (plane, p, c, zl))

    def swap_over(self, value):
        return self.permute(value, lambda plane, c, p, zl: (plane, p, 1 - c, zl))

    def send_shard(self, shard):
        return self.swap(shard), self.swap_over(shard)

    def line_up(self, shards, p):
        one, two = shards
        return jnp.where(p == 0, jnp.concatenate([one, two]), jnp.concatenate([two, one]))

    def sum_quad(self, value):
        value = value + self.core(value)
        return value + self.pair(value)

    def sum_quads(self, value):
        value = value + self.permute(value, lambda plane, c, p, zl: (plane, c, 1 - p, zl))
        step = 1
        while step < self.planes:
            value = value + self.plane_step(value, step)
            step *= 2
        return value

    def swap_over_back(self, value):
        return self.permute(value, lambda plane, c, p, zl: (plane, 1 - p, c, zl))

    def flip(self, value, into):
        pairs = []
        for plane in range(self.planes):
            for c in range(2):
                for zl in range(2):
                    near, far = self.number(plane, c, c, zl), self.number(plane, c, 1 - c, zl)
                    pairs.append((far, near) if into else (near, far))
        return lax.ppermute(value, AXES, pairs)

    def core(self, value):
        return self.permute(value, lambda plane, c, p, zl: (plane, 1 - c, p, zl))

    def pair(self, value):
        return self.permute(value, lambda plane, c, p, zl: (plane, c, p, 1 - zl))

    def plane_step(self, value, flip):
        return self.permute(value, lambda plane, c, p, zl: (plane ^ flip, c, p, zl))

    def both(self, shard, other, c):
        return jnp.where(c == 0, jnp.concatenate([shard, other]), jnp.concatenate([other, shard]))

    def gather(self, block):
        return lax.all_gather(block, "dp", axis=0, tiled=True, axis_index_groups=self.groups)

    def gather_near(self, block):
        if self.planes != 4:
            return (self.gather(block),)
        return block, self.plane_step(block, 1), self.plane_step(block, 2)

    def far_sends(self, pieces):
        if self.planes != 4:
            return ()
        half = pieces[0].shape[0] // 2
        return pieces[1][:half], pieces[2][half:]

    def gather_far(self, pieces, sends):
        if self.planes != 4:
            return pieces
        return *pieces, self.plane_step(sends[0], 2), self.plane_step(sends[1], 1)

    def assemble(self, pieces, plane):
        if self.planes != 4:
            return pieces[0]
        block, across, along, far_one, far_two = pieces
        rows = block.shape[0]
        whole = jnp.zeros((4 * rows, block.shape[1]), block.dtype)
        put = lambda whole, piece, place: lax.dynamic_update_slice(whole, piece, (place, 0))
        whole = put(whole, block, plane * rows)
        whole = put(whole, across, (plane ^ 1) * rows)
        whole = put(whole, along, (plane ^ 2) * rows)
        whole = put(whole, far_one, (plane ^ 3) * rows)
        return put(whole, far_two, (plane ^ 3) * rows + rows // 2)

    def scatter(self, grad):
        return lax.psum_scatter(grad, "dp", scatter_dimension=0, tiled=True, axis_index_groups=self.groups)

    def near_sends(self, grad, plane):
        if self.planes != 4:
            return ()
        rows = grad.shape[0] // 4
        half = rows // 2
        take = lambda place: lax.dynamic_slice(grad, (place, 0), (half, grad.shape[1]))
        return take((plane ^ 3) * rows), take((plane ^ 3) * rows + half)

    def scatter_near(self, grad, sends):
        if self.planes != 4:
            return self.scatter(grad)
        return self.plane_step(sends[0], 1), self.plane_step(sends[1], 2)

    def later_sends(self, grad, got, plane):
        if self.planes != 4:
            return ()
        rows = grad.shape[0] // 4
        half = rows // 2
        take = lambda place, count: lax.dynamic_slice(grad, (place, 0), (count, grad.shape[1]))
        add = lambda left, right: (left.astype(F32) + right.astype(F32)).astype(BF16)
        to_across = jnp.concatenate(
            [take((plane ^ 1) * rows, half), add(take((plane ^ 1) * rows + half, half), got[1])]
        )
        to_along = jnp.concatenate(
            [add(take((plane ^ 2) * rows, half), got[0]), take((plane ^ 2) * rows + half, half)]
        )
        return to_across, to_along

    def scatter_far(self, grad, got, sends, plane):
        if self.planes != 4:
            return got
        rows = grad.shape[0] // 4
        mine = lax.dynamic_slice(grad, (plane * rows, 0), (rows, grad.shape[1]))
        return mine, self.plane_step(sends[0], 1), self.plane_step(sends[1], 2)

    def scatter_sum(self, parts):
        if self.planes != 4:
            return parts
        return sum([part.astype(F32) for part in parts]).astype(BF16)

    def own_shards(self, part, received, c):
        whole = part.astype(F32) + received.astype(F32)
        first, second = jnp.split(whole, 2)
        return jnp.where(c == 0, first, second), jnp.where(c == 0, second, first)


def hold(*values):
    return lax.optimization_barrier(values)


def after(value, *others):
    return lax.optimization_barrier((value, others))[0]


def on_device(
    tokens,
    cotangent,
    lengths,
    granularity,
    ln1_gain,
    ln1_bias,
    w_qkv,
    w_out,
    ln2_gain,
    ln2_bias,
    w_up,
    w_down,
):
    layout = Layout(lax.axis_size("dp"), lax.axis_size("mp"))
    slots = 4
    dp_index, mp_index = lax.axis_index("dp"), lax.axis_index("mp")
    c, p, zl = dp_index % 2, mp_index // 2, mp_index % 2
    plane = dp_index // 2
    index = 2 * c + zl
    rows = tokens.shape[0]
    total = slots * rows
    part_width = w_qkv.shape[2]
    heads = part_width // HDIM
    units = w_up.shape[1]

    facts = jnp.concatenate([lengths[0], granularity])
    other_facts = layout.core(facts)
    facts = jnp.where(p == c, facts, other_facts)
    piece_lengths, piece_gran = facts[:-1], facts[-1]

    depth = w_qkv.shape[0]
    w_qkv_flat, _ = hold(w_qkv.reshape(depth, -1), other_facts)
    sent_qkv = layout.send_shard(w_qkv_flat)
    block_qkv = layout.line_up(sent_qkv, p)
    wide_qkv = layout.gather(block_qkv)
    moved_tokens = layout.swap(after(tokens, block_qkv))
    sent_out = layout.send_shard(after(w_out, block_qkv))
    other_down = layout.core(after(w_down, block_qkv))
    both_down = layout.both(w_down, other_down, c)

    slot_of = jnp.arange(total, dtype=jnp.int32) // rows
    places = (slot_of ^ index) * rows + jnp.arange(total, dtype=jnp.int32) % rows
    seg_ends = jnp.cumsum(piece_lengths)
    starts = seg_ends - piece_lengths
    seg_ids = jnp.sum((places[:, None] >= seg_ends[None, :]).astype(jnp.int32), axis=1)
    member = seg_ids[:, None] == jnp.arange(piece_lengths.shape[0], dtype=jnp.int32)[None, :]
    start = jnp.sum(jnp.where(member, starts[None, :], 0), axis=1)
    half = HDIM // 2
    frequencies = jnp.exp(jnp.arange(half, dtype=F32) * (-2.0 * math.log(10000.0) / HDIM))
    angles = (places - start).astype(F32)[:, None] * frequencies[None, :]
    cosine, sine = jnp.cos(angles), jnp.sin(angles)
    cosine = jnp.concatenate([cosine, cosine], axis=1)
    sine = jnp.concatenate([-sine, sine], axis=1)
    start = start[:, None]
    where = index[None]

    moved_tokens, cosine, sine, start, both_down = hold(moved_tokens, cosine, sine, start, both_down)
    pair_tokens = layout.pair(moved_tokens)
    block_out = layout.line_up(after(sent_out, moved_tokens), p)
    wide_out = layout.gather(block_out)
    pair_tokens, block_out = hold(pair_tokens, block_out)
    near_tokens = jnp.concatenate([moved_tokens, pair_tokens]).astype(F32)
    near_one, unit_one, inverse_one = norm_forward(near_tokens, ln1_gain, ln1_bias)
    near_one, w_up = hold(near_one.astype(BF16), w_up)
    sent_up = layout.send_shard(w_up)
    inputs_one = jnp.concatenate([near_one, layout.core(near_one)])
    projected = dot_nn(inputs_one, wide_qkv)
    projected, sent_up, both_down = hold(projected, sent_up, both_down)
    block_up, projected, both_down = hold(layout.line_up(sent_up, p), projected, both_down)
    pieces_up = layout.gather_near(block_up)
    flip_down = layout.flip(both_down, False)
    mixed, q_all, k_all, v_all, lse = attend(where, projected, cosine, sine, start, heads, slots)
    attn_part = dot_nn(mixed, wide_out)
    attn_send = attn_part[2 * rows :].astype(BF16)
    attn_send, pieces_up, flip_down = hold(attn_send, pieces_up, flip_down)

    attn_got, pieces_up, flip_down = hold(layout.core(attn_send), pieces_up, flip_down)
    attn_chip = attn_part[: 2 * rows] + attn_got.astype(F32)
    attn_low, pieces_up, flip_down, cotangent = hold(attn_chip.astype(BF16), pieces_up, flip_down, cotangent)
    attn_other = layout.pair(attn_low)
    block_down = jnp.where(p == c, both_down, flip_down)
    wide_down = layout.gather(block_down)
    pieces_up = layout.gather_far(pieces_up, layout.far_sends(pieces_up))
    moved_cot = layout.swap(cotangent)
    attn_other, pieces_up, moved_cot, block_down = hold(attn_other, pieces_up, moved_cot, block_down)

    def pair_order(other):
        other = other.astype(F32)
        return jnp.concatenate([other[rows:], other[:rows]])

    resid_one = near_tokens + attn_chip + pair_order(attn_other)
    near_two, unit_two, inverse_two = norm_forward(resid_one, ln2_gain, ln2_bias)
    near_two, pieces_up, moved_cot = hold(near_two.astype(BF16), pieces_up, moved_cot)
    pair_cot = layout.pair(moved_cot)
    inputs_two = jnp.concatenate([near_two, layout.core(near_two)])
    wide_up = layout.assemble(pieces_up, plane)

    prefix = PREFIX0 * jnp.left_shift(jnp.int32(1), piece_gran)
    active_units = jnp.clip(prefix - index * units, 0, units)
    keep_units = (jnp.arange(units, dtype=jnp.int32) < active_units).astype(F32)
    pre_act = dot_nn(inputs_two, wide_up)
    hidden_act = (jax.nn.gelu(pre_act, approximate=True) * keep_units).astype(BF16)
    hidden_act, pair_cot = hold(hidden_act, pair_cot)
    near_cot = jnp.concatenate([moved_cot, pair_cot])
    cot_all = jnp.concatenate([near_cot, layout.core(near_cot)])
    grad_down_part = dot_tn(hidden_act, cot_all).astype(BF16)
    grad_down_sum = layout.scatter(grad_down_part)
    wide_down = after(wide_down, grad_down_part)
    hidden_grad = dot_nt(cot_all, wide_down)
    pre_grad = (gelu_back(pre_act, hidden_grad) * keep_units).astype(BF16)
    ffn_part = dot_nt(pre_grad, wide_up)
    (ffn_send,) = hold(ffn_part[2 * rows :].astype(BF16))
    (ffn_got,) = hold(layout.core(ffn_send))
    ffn_chip = ffn_part[: 2 * rows] + ffn_got.astype(F32)
    ffn_low, pre_grad, hidden_act = hold(ffn_chip.astype(BF16), pre_grad, hidden_act)
    ffn_other = layout.pair(ffn_low)
    grad_up_part = dot_tn(inputs_two, pre_grad).astype(BF16)
    grad_up_sum = layout.scatter(grad_up_part)
    out_part = dot_nn(hidden_act, wide_down)
    out_send = out_part[2 * rows :].astype(BF16)
    ffn_other, out_send, grad_up_part = hold(ffn_other, out_send, grad_up_part)
    near_two_grad = ffn_chip + pair_order(ffn_other)

    resid_grad = near_cot.astype(F32) + norm_backward(near_two_grad, unit_two, inverse_two, ln2_gain)
    resid_low = resid_grad.astype(BF16)
    resid_low, out_send, down_sum = hold(resid_low, out_send, grad_down_sum)
    down_flip = layout.flip(down_sum, True)
    out_got = layout.core(out_send)
    resid_all = jnp.concatenate([resid_low, layout.core(resid_low)])
    mixed_grad = dot_nt(resid_all, wide_out).astype(BF16)
    out_got = after(out_got, mixed_grad)
    out_send = (out_part[rows : 2 * rows] + out_got[rows:].astype(F32)).astype(BF16)
    out_other = layout.pair(out_send)
    projected_grad = attend_back(
        where, after(mixed_grad, out_send), q_all, k_all, v_all, lse, cosine, sine, start, heads, slots
    )
    grad_qkv_part = dot_tn(inputs_one, projected_grad).astype(BF16)
    near_qkv = layout.near_sends(grad_qkv_part, plane)
    near_qkv, down_flip, out_other, projected_grad = hold(near_qkv, down_flip, out_other, projected_grad)

    got_qkv = layout.scatter_near(grad_qkv_part, near_qkv)
    one_part = dot_nt(projected_grad, wide_qkv)
    one_send = one_part[2 * rows :].astype(BF16)
    grad_out_part = dot_tn(mixed, after(resid_all, one_send)).astype(BF16)
    one_send, got_qkv, grad_out_part = hold(one_send, got_qkv, grad_out_part)
    grad_out_sum = layout.scatter(grad_out_part)
    one_got = layout.core(one_send)
    output = resid_one[:rows] + out_part[:rows] + out_got[:rows].astype(F32) + after(out_other, one_send).astype(F32)
    one_got, output = hold(one_got, output.astype(BF16))
    one_send = (one_part[rows : 2 * rows] + one_got[rows:].astype(F32)).astype(BF16)
    one_send, got_qkv, output, near_two_grad, up_sum = hold(one_send, got_qkv, output, near_two_grad, grad_up_sum)
    one_other = layout.pair(one_send)
    later_qkv = layout.later_sends(grad_qkv_part, got_qkv, plane)
    qkv_parts = layout.scatter_far(grad_qkv_part, got_qkv, later_qkv, plane)
    up_flip = layout.flip(up_sum, True)
    moved_output = layout.swap(output)
    one_other, qkv_parts, up_flip, moved_output, near_two_grad = hold(
        one_other, qkv_parts, up_flip, moved_output, near_two_grad
    )

    own_one_grad = one_part[:rows] + one_got[:rows].astype(F32) + one_other.astype(F32)
    norm_parts = [
        jnp.sum(own_one_grad * unit_one[:rows], axis=0),
        jnp.sum(own_one_grad, axis=0),
        jnp.sum(near_two_grad[:rows] * unit_two[:rows], axis=0),
        jnp.sum(near_two_grad[:rows], axis=0),
    ]
    input_grad = resid_grad[:rows] + norm_backward(own_one_grad, unit_one[:rows], inverse_one[:rows], ln1_gain)
    input_grad, norm_parts, qkv_parts = hold(input_grad.astype(BF16), jnp.stack(norm_parts), qkv_parts)
    moved_input = layout.swap(input_grad)
    norm_parts = layout.sum_quad(norm_parts)
    qkv_sum = layout.scatter_sum(qkv_parts)
    one_sum = jnp.concatenate([qkv_sum, grad_out_sum.reshape(qkv_sum.shape[0], -1)], axis=1)
    norm_parts, one_sum, moved_input = hold(norm_parts, one_sum, moved_input)
    down_own, down_other = layout.own_shards(down_sum, down_flip, c)
    first, second = jnp.split(one_sum, 2)
    one_own = layout.swap(jnp.where(p == 0, first, second))
    one_far = layout.swap_over_back(jnp.where(p == 0, second, first))
    norm_sums = layout.sum_quads(norm_parts)
    up_own, up_other = layout.own_shards(up_sum, up_flip, c)
    down_got, up_got = layout.core(down_other), layout.core(up_other)
    grad_down = jnp.where(p == c, down_own, down_got)
    grad_up = jnp.where(p == c, up_own, up_got)
    one_own, one_far, norm_sums, grad_down, grad_up = hold(one_own, one_far, norm_sums, grad_down, grad_up)
    lanes = lambda part: slice(part * part_width, (part + 1) * part_width)
    total_of = lambda part: one_own[:, lanes(part)].astype(F32) + one_far[:, lanes(part)].astype(F32)
    grad_qkv = jnp.stack([total_of(0), total_of(1), total_of(2)], axis=1)
    grad_out = total_of(3).reshape(w_out.shape)
    output, input_grad = moved_output, moved_input
    return (
        output,
        input_grad,
        norm_sums[0],
        norm_sums[1],
        grad_qkv.reshape(w_qkv.shape),
        grad_out,
        norm_sums[2],
        norm_sums[3],
        grad_up,
        grad_down,
    )


def solution(mesh):
    return jax.shard_map(
        on_device,
        mesh=mesh,
        in_specs=(
            P(("dp", "mp"), None),
            P(("dp", "mp"), None),
            P("dp", None),
            P("dp"),
            P(),
            P(),
            P("dp", None, "mp"),
            P(("mp", "dp"), None),
            P(),
            P(),
            P("dp", "mp"),
            P(("mp", "dp"), None),
        ),
        out_specs=(
            P(("dp", "mp"), None),
            P(("dp", "mp"), None),
            P(),
            P(),
            P("dp", None, "mp"),
            P(("mp", "dp"), None),
            P(),
            P(),
            P("dp", "mp"),
            P(("mp", "dp"), None),
        ),
        check_vma=False,
    )
```
